256 devices in a mesh: seq: 32 (over y, z), mp: 8 (over x, core).
Axes of the slice: x: 4, y: 4, z: 8, core: 2. Of those that a mesh axis runs over, the one named last changes fastest.
Arguments:
- query_rows: bfloat16 [16384, 8192], P('seq', 'mp'), may hold values from -8 to 8
- key_rows: bfloat16 [16384, 1024], P('seq', 'mp'), may hold values from -8 to 8
- value_rows: bfloat16 [16384, 1024], P('seq', 'mp'), may hold values from -6 to 6
- cotangent: bfloat16 [16384, 8192], P('seq', 'mp'), may hold values from -6 to 6
- router_logits: float32 [16384], P('seq'), may hold values from -8 to 8
- selection: int32 [4096], P('seq'), may hold values from -1 to 511, as said below
Outputs:
- mixed: bfloat16 [16384, 8192], P('seq', 'mp')
- query_grad: bfloat16 [16384, 8192], P('seq', 'mp')
- key_grad: bfloat16 [16384, 1024], P('seq', 'mp')
- value_grad: bfloat16 [16384, 1024], P('seq', 'mp')
- router_grad: float32 [16384], P('seq')
The draws below stay inside these ranges and needn't reach their ends.
Inputs may be any that keep to these rules, and one draw needn't show every extreme that they name: `selection`: each shard's block of 128 entries lists the local positions of its selected tokens in ascending order, then -1 in the remaining entries; all shards together select exactly 2048 tokens, and some shard selects exactly 128.
All inputs are finite; a program needn't handle non-finite values.
Results may differ from the reference program's by a relative error of at most 0.012.
The reference program's roundings to bfloat16 on the way count: a program that leaves them out, or rounds other values in their place, can miss the bound.
Values may be sent and summed in bfloat16 or wider, within the bound.
No kernel may reach another device: no remote copies, remote signals or barrier semaphores. Data moves between devices by JAX's collectives and lax.ppermute only.
A program may use at most 64 MiB of HBM per device.

```python
import jax
import jax.numpy as jnp
from jax import lax

HEADS = 64
KV_HEADS = 8
HEAD_DIM = 128
TOK_DEV = 512
SEL_DEV = 64
SLOTS = 128
LEN = 16384
SELECTED = 2048
N_SEQ = 32


def shard_counts(key):
    shuffled = jax.random.permutation(jax.random.fold_in(key, 101), N_SEQ)
    shifts = jax.random.randint(jax.random.fold_in(key, 102), (N_SEQ // 2,), 0, SEL_DEV)
    shifts = shifts.at[0].set(SEL_DEV)
    deltas = jnp.stack([shifts, -shifts], axis=1).reshape(-1)
    return jnp.zeros((N_SEQ,), jnp.int32).at[shuffled].set((SEL_DEV + deltas).astype(jnp.int32))


def draw_selection(key, part):
    counts = shard_counts(key)

    def one_shard(shard_key, chosen_count):
        shuffled = jax.random.permutation(shard_key, TOK_DEV)
        rank_of = jnp.argsort(shuffled)
        chosen = rank_of < chosen_count
        position_ids = jnp.arange(TOK_DEV, dtype=jnp.int32)
        ordered = jnp.argsort(jnp.where(chosen, position_ids, TOK_DEV + position_ids))[:SLOTS]
        return jnp.where(jnp.arange(SLOTS) < chosen_count, ordered, -1).astype(jnp.int32)
    shard_keys = jax.random.split(jax.random.fold_in(key, 103), N_SEQ)
    return jax.vmap(one_shard)(shard_keys, counts).reshape(-1)


def draw_query_rows(key, part):
    own = jax.random.fold_in(key, 11)
    shape = (LEN, HEADS * HEAD_DIM)
    values = jnp.clip(1.5 * jax.random.normal(own, shape), -8.0, 8.0)
    return values.astype(jnp.bfloat16)


def draw_key_rows(key, part):
    own = jax.random.fold_in(key, 13)
    shape = (LEN, KV_HEADS * HEAD_DIM)
    values = jnp.clip(1.4 * jax.random.normal(own, shape), -8.0, 8.0)
    return values.astype(jnp.bfloat16)


def block_levels(key, dims, shards, least, high):
    def one(dim, shards_of):
        draws = jax.random.uniform(jax.random.fold_in(jax.random.fold_in(key, 6), dim), (shards_of,), jnp.float32, least / len(shards), high / len(shards))
        return jnp.repeat(jnp.exp(draws), dims[dim] // shards_of).reshape((-1,) + (1,) * (len(dims) - dim - 1))

    factor_of = one(*shards[0])
    for cut in shards[1:]:
        factor_of = factor_of * one(*cut)
    return factor_of


def gaussian(rng, extent, deviation, limit, shards=(), held_as=jnp.bfloat16):
    entries = deviation * jax.random.normal(rng, extent, jnp.float32)
    if shards:
        entries = entries * block_levels(rng, extent, shards, -0.22, 0.18)
    return jnp.clip(entries, -limit, limit).astype(held_as)


def setup_inputs(seed: int = 0) -> dict:
    arg_keys = jax.random.split(jax.random.key(seed), 7)
    query_rows = draw_query_rows(jax.random.fold_in(arg_keys[6], 71), 0)
    key_rows = draw_key_rows(jax.random.fold_in(arg_keys[6], 71), 0)
    value_rows = gaussian(arg_keys[2], (LEN, KV_HEADS * HEAD_DIM), 1.0, 6.0, ((0, 32), (1, 8)))
    cotangent = gaussian(arg_keys[3], (LEN, HEADS * HEAD_DIM), 1.0, 6.0, ((0, 32), (1, 8)))
    router_logits = gaussian(arg_keys[4], (LEN,), 2.0, 8.0, ((0, 32),), jnp.float32)
    selection = draw_selection(jax.random.fold_in(arg_keys[6], 71), 0)
    return dict(query_rows=query_rows, key_rows=key_rows, value_rows=value_rows, cotangent=cotangent, router_logits=router_logits, selection=selection)


def group_pass(kv_head, q_sel, k_sel, v_sel, grad_sel):
    group = HEADS // KV_HEADS
    scale = HEAD_DIM ** -0.5
    start_col = (kv_head * HEAD_DIM).astype(jnp.int32)
    key_head = lax.dynamic_slice_in_dim(k_sel, start_col, HEAD_DIM, 1)
    value_head = lax.dynamic_slice_in_dim(v_sel, start_col, HEAD_DIM, 1)
    rank_ids = jnp.arange(SELECTED, dtype=jnp.int32)
    allowed = rank_ids[None, :] <= rank_ids[:, None]
    outputs, query_grads = [], []
    key_acc = jnp.zeros((SELECTED, HEAD_DIM), jnp.float32)
    value_acc = jnp.zeros((SELECTED, HEAD_DIM), jnp.float32)
    for member in range(group):
        col_start = ((kv_head * group + member) * HEAD_DIM).astype(jnp.int32)
        query_head = lax.dynamic_slice_in_dim(q_sel, col_start, HEAD_DIM, 1)
        grad_head = lax.dynamic_slice_in_dim(grad_sel, col_start, HEAD_DIM, 1)
        scores = jnp.dot(query_head, key_head.T, preferred_element_type=jnp.float32) * scale
        top_score = jnp.max(jnp.where(allowed, scores, -jnp.inf), axis=1, keepdims=True)
        expo = jnp.where(allowed, jnp.exp(scores - top_score), 0.0)
        weights = (expo / jnp.sum(expo, axis=1, keepdims=True)).astype(jnp.bfloat16)
        attended = jnp.dot(weights, value_head, preferred_element_type=jnp.float32).astype(jnp.bfloat16)
        slope = jnp.dot(grad_head, value_head.T, preferred_element_type=jnp.float32)
        centre = jnp.sum(grad_head.astype(jnp.float32) * attended.astype(jnp.float32), axis=1, keepdims=True)
        d_scores = (weights.astype(jnp.float32) * (slope - centre) * scale).astype(jnp.bfloat16)
        query_grads.append(jnp.dot(d_scores, key_head, preferred_element_type=jnp.float32).astype(jnp.bfloat16))
        key_acc = key_acc + jnp.dot(d_scores.T, query_head, preferred_element_type=jnp.float32)
        value_acc = value_acc + jnp.dot(weights.T, grad_head, preferred_element_type=jnp.float32)
        outputs.append(attended)
    return (jnp.concatenate(outputs, axis=1), jnp.concatenate(query_grads, axis=1),
            key_acc.astype(jnp.bfloat16), value_acc.astype(jnp.bfloat16))


def reference(query_rows, key_rows, value_rows, cotangent, router_logits, selection):
    table = selection.reshape(N_SEQ, SLOTS)
    picked = table >= 0
    counts = jnp.sum(picked.astype(jnp.int32), axis=1).astype(jnp.int32)
    offsets = (jnp.cumsum(counts) - counts).astype(jnp.int32)
    ranks = offsets[:, None] + jnp.arange(SLOTS, dtype=jnp.int32)[None, :]
    global_pos = jnp.arange(N_SEQ, dtype=jnp.int32)[:, None] * TOK_DEV + jnp.maximum(table, 0)
    target = jnp.where(picked, ranks, SELECTED).reshape(-1).astype(jnp.int32)
    order = jnp.zeros((SELECTED,), jnp.int32).at[target].set(global_pos.reshape(-1).astype(jnp.int32), mode="drop")
    q_sel = query_rows[order]
    k_sel = key_rows[order]
    v_sel = value_rows[order]
    cot_sel = cotangent[order]
    router = jax.nn.sigmoid(router_logits[order].astype(jnp.float32))
    grad_sel = (router[:, None] * cot_sel.astype(jnp.float32)).astype(jnp.bfloat16)

    def one_group(kv_head):
        return group_pass(kv_head, q_sel, k_sel, v_sel, grad_sel)

    attended, dq_sel, dk_sel, dv_sel = lax.map(one_group, jnp.arange(KV_HEADS, dtype=jnp.int32))
    attended = jnp.transpose(attended, (1, 0, 2)).reshape(SELECTED, HEADS * HEAD_DIM)
    dq_sel = jnp.transpose(dq_sel, (1, 0, 2)).reshape(SELECTED, HEADS * HEAD_DIM)
    dk_sel = jnp.transpose(dk_sel, (1, 0, 2)).reshape(SELECTED, KV_HEADS * HEAD_DIM)
    dv_sel = jnp.transpose(dv_sel, (1, 0, 2)).reshape(SELECTED, KV_HEADS * HEAD_DIM)
    out_f = attended.astype(jnp.float32)
    mixed = jnp.zeros((LEN, HEADS * HEAD_DIM), jnp.bfloat16).at[order].set((router[:, None] * out_f).astype(jnp.bfloat16))
    query_grad = jnp.zeros((LEN, HEADS * HEAD_DIM), jnp.bfloat16).at[order].set(dq_sel)
    key_grad = jnp.zeros((LEN, KV_HEADS * HEAD_DIM), jnp.bfloat16).at[order].set(dk_sel)
    value_grad = jnp.zeros((LEN, KV_HEADS * HEAD_DIM), jnp.bfloat16).at[order].set(dv_sel)
    feature_sum = jnp.sum(cot_sel.astype(jnp.float32) * out_f, axis=1)
    router_grad = jnp.zeros((LEN,), jnp.float32).at[order].set(router * (1.0 - router) * feature_sum)
    return mixed, query_grad, key_grad, value_grad, router_grad
```

```python
import functools

import jax
import jax.numpy as jnp
from jax import lax
from jax.experimental import pallas as pl
from jax.experimental.pallas import tpu as pltpu
from jax.sharding import Mesh, PartitionSpec as P

HEAD_DIM = 128
SLOTS = 128
TOK = 512
HEADS = 8
ROWS_Y = 4
ROWS_Z = 8
LANES = HEADS * HEAD_DIM
KEYS = ROWS_Y * ROWS_Z * SLOTS
TILE = 256
QCHUNK = 256
FLAG = 64.0
NEG = -1e30
SCALE = HEAD_DIM ** (-0.5)
LOG2E = 1.4426950408889634
BF = jnp.bfloat16
F32 = jnp.float32
NT = (((1,), (1,)), ((), ()))
NN = (((1,), (0,)), ((), ()))
VMEM = pltpu.VMEM
LIMIT = 60 * 1024 * 1024


def dot(a, b, dims=NN):
    return lax.dot_general(a, b, dims, preferred_element_type=F32)


def column_of(row):
    return jnp.transpose(jnp.broadcast_to(row, (SLOTS, SLOTS)))


def picker(sel_row):
    col = column_of(sel_row.astype(F32))
    lane = lax.broadcasted_iota(jnp.int32, (SLOTS, SLOTS), 1).astype(F32)
    return jnp.concatenate([col == lane + float(c * SLOTS) for c in range(TOK // SLOTS)], axis=1)


def placer(sel_row):
    token = lax.broadcasted_iota(jnp.int32, (TOK, SLOTS), 0)
    return jnp.broadcast_to(sel_row, (TOK, SLOTS)) == token


def one_hot(mask):
    return jnp.where(mask, 1.0, 0.0).astype(BF)


def select_kv_kernel(sel_ref, key_ref, value_ref, out_ref):
    sel = sel_ref[...]
    pick = one_hot(picker(sel))
    live = column_of(sel.astype(F32)) >= 0.0
    key = jnp.where(live, dot(pick, key_ref[...]), FLAG).astype(BF)
    value = dot(pick, value_ref[...]).astype(BF)
    for copy in range(ROWS_Z):
        out_ref[copy, :, :HEAD_DIM] = key
        out_ref[copy, :, HEAD_DIM:] = value


def select_q_kernel(sel_ref, logit_ref, query_ref, cot_ref, q_ref, g_ref, c_ref, router_ref):
    mask = picker(sel_ref[...])
    pick = one_hot(mask)
    logit = jnp.sum(jnp.where(mask, logit_ref[...], 0.0), axis=1, keepdims=True)
    router = 1.0 / (1.0 + jnp.exp(-logit))
    router_ref[...] = jnp.broadcast_to(router, (SLOTS, SLOTS))
    for h in range(HEADS):
        cols = slice(h * HEAD_DIM, (h + 1) * HEAD_DIM)
        rows = slice(h * SLOTS, (h + 1) * SLOTS)
        q_ref[rows, :] = dot(pick, query_ref[:, cols]).astype(BF)
        cot = dot(pick, cot_ref[:, cols])
        c_ref[rows, :] = cot.astype(BF)
        g_ref[rows, :] = (router * cot).astype(BF)


def attention_kernel(pos_ref, kv0, kv1, kv2, kv3, q_ref, g_ref, c_ref,
                     att_ref, dq_ref, dkv_ref, feat_ref,
                     kvs, s_ref, w_ref, at_ref, dqt_ref, top_ref, sum_ref, cen_ref, sem):
    row = pos_ref[0]
    col = pos_ref[1]
    block = ROWS_Z * SLOTS
    copies = []
    for k, src in enumerate((kv0, kv1, kv2, kv3)):
        owner = lax.rem(row - k + ROWS_Y, ROWS_Y)
        start = pl.multiple_of(owner * block, block)
        copies.append(pltpu.make_async_copy(src, kvs.at[pl.ds(start, block), :], sem.at[k]))
    for c in copies:
        c.start()
    at_ref[...] = jnp.zeros_like(at_ref)
    dqt_ref[...] = jnp.zeros_like(dqt_ref)
    top_ref[...] = jnp.full_like(top_ref, NEG)
    sum_ref[...] = jnp.zeros_like(sum_ref)
    tiles = row * (block // TILE) + col * SLOTS // TILE + 1
    query_id = (row * ROWS_Z + col) * SLOTS
    for c in copies:
        c.wait()

    def scores(t, carry):
        keys = kvs[pl.ds(pl.multiple_of(t * TILE, TILE), TILE), :HEAD_DIM]
        kid = t * TILE + lax.broadcasted_iota(jnp.int32, (TILE, SLOTS), 0)
        qid = query_id + lax.broadcasted_iota(jnp.int32, (TILE, SLOTS), 1)
        dead = jnp.broadcast_to(keys[:, :1].astype(F32), (TILE, SLOTS)) > 0.5 * FLAG
        bias = jnp.where((kid > qid) | dead, NEG, 0.0)
        bias = jnp.concatenate([bias] * (QCHUNK // SLOTS), axis=1)
        for c in range(LANES // QCHUNK):
            lanes = slice(c * QCHUNK, (c + 1) * QCHUNK)
            s = dot(keys, q_ref[lanes, :], NT) * (SCALE * LOG2E) + bias
            s_ref[pl.ds(pl.multiple_of(t * TILE, TILE), TILE), lanes] = s
            part = jnp.max(s.reshape(TILE // 8, 8, QCHUNK), axis=0)
            top_ref[:, lanes] = jnp.maximum(top_ref[:, lanes], part)
        return carry

    lax.fori_loop(0, tiles, scores, 0)
    top_ref[...] = jnp.broadcast_to(jnp.max(top_ref[...], axis=0, keepdims=True), top_ref.shape)

    def exponent(t, carry):
        rows = pl.ds(pl.multiple_of(t * TILE, TILE), TILE)
        for c in range(LANES // QCHUNK):
            lanes = slice(c * QCHUNK, (c + 1) * QCHUNK)
            e = jnp.exp2(s_ref[rows, lanes] - top_ref[:1, lanes])
            s_ref[rows, lanes] = e
            sum_ref[:, lanes] += jnp.sum(e.reshape(TILE // 8, 8, QCHUNK), axis=0)
        return carry

    lax.fori_loop(0, tiles, exponent, 0)
    total = jnp.sum(sum_ref[...], axis=0, keepdims=True)
    sum_ref[...] = jnp.broadcast_to(1.0 / total, sum_ref.shape)

    def forward(t, carry):
        rows = pl.ds(pl.multiple_of(t * TILE, TILE), TILE)
        value_t = jnp.transpose(kvs[rows, HEAD_DIM:])
        for c in range(LANES // QCHUNK):
            lanes = slice(c * QCHUNK, (c + 1) * QCHUNK)
            w = (s_ref[rows, lanes] * sum_ref[:1, lanes]).astype(BF)
            w_ref[rows, lanes] = w
            at_ref[:, lanes] += dot(value_t, w)
        dkv_ref[rows, HEAD_DIM:] = dot(w_ref[rows, :], g_ref[...]).astype(BF)
        return carry

    lax.fori_loop(0, tiles, forward, 0)

    feature = jnp.zeros((SLOTS, HEAD_DIM), F32)
    for h in range(HEADS):
        lanes = slice(h * HEAD_DIM, (h + 1) * HEAD_DIM)
        att_t = at_ref[:, lanes].astype(BF)
        att = jnp.transpose(att_t)
        att_ref[:, lanes] = att
        grad_t = jnp.transpose(g_ref[lanes, :])
        centre = jnp.sum(grad_t.astype(F32) * att_t.astype(F32), axis=0, keepdims=True)
        cen_ref[:, lanes] = jnp.broadcast_to(centre, (8, HEAD_DIM))
        feature += c_ref[lanes, :].astype(F32) * att.astype(F32)
    feature = jnp.broadcast_to(jnp.sum(feature, axis=1, keepdims=True), (SLOTS, SLOTS))
    feature = jnp.transpose(feature)[:8, :]
    for peer in range(8):
        feat_ref[peer] = feature

    def backward(t, carry):
        rows = pl.ds(pl.multiple_of(t * TILE, TILE), TILE)
        values = kvs[rows, HEAD_DIM:]
        key_t = jnp.transpose(kvs[rows, :HEAD_DIM])
        acc = jnp.zeros((TILE, HEAD_DIM), F32)
        for c in range(LANES // QCHUNK):
            lanes = slice(c * QCHUNK, (c + 1) * QCHUNK)
            slope = dot(values, g_ref[lanes, :], NT)
            ds = (w_ref[rows, lanes].astype(F32) * (slope - cen_ref[:1, lanes]) * SCALE).astype(BF)
            dqt_ref[:, lanes] += dot(key_t, ds)
            acc += dot(ds, q_ref[lanes, :])
        dkv_ref[rows, :HEAD_DIM] = acc.astype(BF)
        return carry

    lax.fori_loop(0, tiles, backward, 0)

    def clear(t, carry):
        dkv_ref[pl.ds(pl.multiple_of(t * TILE, TILE), TILE), :] = jnp.zeros((TILE, 2 * HEAD_DIM), BF)
        return carry

    lax.fori_loop(tiles, KEYS // TILE, clear, 0)
    for h in range(HEADS):
        lanes = slice(h * HEAD_DIM, (h + 1) * HEAD_DIM)
        dq_ref[:, lanes] = jnp.transpose(dqt_ref[:, lanes].astype(BF))


def place_q_kernel(sel_ref, router_ref, att_ref, dq_ref, mixed_ref, qgrad_ref):
    place = one_hot(placer(sel_ref[...]))
    router = router_ref[...]
    for h in range(HEADS):
        lanes = slice(h * HEAD_DIM, (h + 1) * HEAD_DIM)
        mix = (router * att_ref[:, lanes].astype(F32)).astype(BF)
        mixed_ref[:, lanes] = dot(place, mix).astype(BF)
        qgrad_ref[:, lanes] = dot(place, dq_ref[:, lanes]).astype(BF)


def add_rows_kernel(in_ref, out_ref):
    total = in_ref[0].astype(F32)
    for k in range(1, ROWS_Y):
        total += in_ref[k].astype(F32)
    out_ref[...] = total.astype(BF)


def place_kv_kernel(sel_ref, router_ref, feat_ref, part_ref, kgrad_ref, vgrad_ref, rgrad_ref):
    total = part_ref[0].astype(F32)
    for k in range(1, ROWS_Z):
        total += part_ref[k].astype(F32)
    placed = dot(one_hot(placer(sel_ref[...])), total.astype(BF)).astype(BF)
    kgrad_ref[...] = placed[:, :HEAD_DIM]
    vgrad_ref[...] = placed[:, HEAD_DIM:]
    feature = feat_ref[0]
    for k in range(1, 8):
        feature += feat_ref[k]
    router = router_ref[...]
    terms = router * (1.0 - router) * column_of(feature[:1, :])
    terms = jnp.concatenate([terms] * (TOK // SLOTS), axis=1)
    rgrad_ref[...] = jnp.sum(jnp.where(picker(sel_ref[...]), terms, 0.0), axis=0, keepdims=True)


def call(kernel, outs, args, scratch=(), specs=None, cost=None):
    return pl.pallas_call(
        kernel,
        out_shape=[jax.ShapeDtypeStruct(s, d) for s, d in outs],
        in_specs=specs or [pl.BlockSpec(memory_space=VMEM)] * len(args),
        out_specs=[pl.BlockSpec(memory_space=VMEM)] * len(outs),
        scratch_shapes=list(scratch),
        compiler_params=pltpu.CompilerParams(vmem_limit_bytes=LIMIT if scratch else 24 * 1024 * 1024),
        cost_estimate=pl.CostEstimate(flops=cost[0], bytes_accessed=cost[1], transcendentals=0),
    )(*args)


def shards(query_rows, key_rows, value_rows, cotangent, router_logits, selection):
    sel = selection.reshape(1, SLOTS)
    logits = router_logits.reshape(1, TOK)
    row = lax.axis_index("y")
    col = lax.axis_index("z")
    (own,) = call(select_kv_kernel, [((ROWS_Z, SLOTS, 2 * HEAD_DIM), BF)], (sel, key_rows, value_rows),
                  cost=(2 * SLOTS * TOK * 256, 1 << 20))
    line = lax.all_to_all(own, "z", 0, 0, tiled=True)
    q, g, c, router = call(
        select_q_kernel,
        [((LANES, HEAD_DIM), BF)] * 3 + [((SLOTS, SLOTS), F32)],
        (sel, logits, query_rows, cotangent),
        cost=(4 * SLOTS * TOK * LANES, 3 << 20))
    line = line.reshape(ROWS_Z * SLOTS, 2 * HEAD_DIM)
    lines = [line] + [
        lax.ppermute(line, "y", [(s, (s + k) % ROWS_Y) for s in range(ROWS_Y)]) for k in range(1, ROWS_Y)
    ]
    pos = jnp.stack([row, col]).astype(jnp.int32)
    specs = [pl.BlockSpec(memory_space=pltpu.SMEM)] + [pl.BlockSpec(memory_space=pl.ANY)] * 4
    specs += [pl.BlockSpec(memory_space=VMEM)] * 3
    att, dq, dkv, feat = call(
        attention_kernel,
        [((SLOTS, LANES), BF), ((SLOTS, LANES), BF), ((KEYS, 2 * HEAD_DIM), BF), ((8, 8, SLOTS), F32)],
        (pos, *lines, q, g, c),
        scratch=[
            VMEM((KEYS, 2 * HEAD_DIM), BF), VMEM((KEYS, LANES), F32), VMEM((KEYS, LANES), BF),
            VMEM((HEAD_DIM, LANES), F32), VMEM((HEAD_DIM, LANES), F32),
            VMEM((8, LANES), F32), VMEM((8, LANES), F32), VMEM((8, LANES), F32),
            pltpu.SemaphoreType.DMA((4,)),
        ],
        specs=specs,
        cost=(12 * KEYS * LANES * HEAD_DIM, 8 << 20))
    feat = lax.all_to_all(feat, "mp", 0, 0, tiled=True)
    part = lax.all_to_all(dkv.reshape(ROWS_Y, ROWS_Z * SLOTS, 2 * HEAD_DIM), "y", 0, 0, tiled=True)
    mixed, qgrad = call(place_q_kernel, [((TOK, LANES), BF)] * 2, (sel, router, att, dq),
                        cost=(4 * SLOTS * TOK * LANES, 3 << 20))
    (part,) = call(add_rows_kernel, [((ROWS_Z * SLOTS, 2 * HEAD_DIM), BF)], (part,),
                   cost=(1 << 20, 3 << 20))
    part = lax.all_to_all(part.reshape(ROWS_Z, SLOTS, 2 * HEAD_DIM), "z", 0, 0, tiled=True)
    kgrad, vgrad, rgrad = call(
        place_kv_kernel,
        [((TOK, HEAD_DIM), BF)] * 2 + [((1, TOK), F32)],
        (sel, router, feat, part),
        cost=(2 * SLOTS * TOK * 256, 1 << 20))
    return mixed, qgrad, kgrad, vgrad, rgrad.reshape(TOK)


def solution(mesh):
    inner = Mesh(mesh.devices.reshape(ROWS_Y, ROWS_Z, 8), ("y", "z", "mp"))
    seq = ("y", "z")
    in_specs = (P(seq, "mp"), P(seq, "mp"), P(seq, "mp"), P(seq, "mp"), P(seq), P(seq))
    out_specs = (P(seq, "mp"), P(seq, "mp"), P(seq, "mp"), P(seq, "mp"), P(seq))
    return jax.shard_map(shards, mesh=inner, in_specs=in_specs, out_specs=out_specs, check_vma=False)
```

```python
import functools

import jax
import jax.numpy as jnp
from jax import lax
from jax.experimental import pallas as pl
from jax.experimental.pallas import tpu as pltpu
from jax.sharding import Mesh, PartitionSpec as P

HEAD_DIM = 128
SLOTS = 128
TOK = 512
HEADS = 8
ROWS_Y = 4
ROWS_Z = 8
LANES = HEADS * HEAD_DIM
KEYS = ROWS_Y * ROWS_Z * SLOTS
TILE = 256
GROUP = 16
SHARDS = ROWS_Y * ROWS_Z
PACKED = 2560
QCHUNK = 256
FLAG = 64.0
NEG = -1e30
SCALE = HEAD_DIM ** (-0.5)
LOG2E = 1.4426950408889634
BF = jnp.bfloat16
F32 = jnp.float32
NT = (((1,), (1,)), ((), ()))
NN = (((1,), (0,)), ((), ()))
VMEM = pltpu.VMEM
LIMIT = 60 * 1024 * 1024


def dot(a, b, dims=NN):
    return lax.dot_general(a, b, dims, preferred_element_type=F32)


def column_of(row):
    return jnp.transpose(jnp.broadcast_to(row, (SLOTS, SLOTS)))


def picker(sel_row):
    col = column_of(sel_row.astype(F32))
    lane = lax.broadcasted_iota(jnp.int32, (SLOTS, SLOTS), 1).astype(F32)
    return jnp.concatenate([col == lane + float(c * SLOTS) for c in range(TOK // SLOTS)], axis=1)


def placer(sel_row):
    token = lax.broadcasted_iota(jnp.int32, (TOK, SLOTS), 0)
    return jnp.broadcast_to(sel_row, (TOK, SLOTS)) == token


def one_hot(mask):
    return jnp.where(mask, 1.0, 0.0).astype(BF)


def select_kv_kernel(sel_ref, key_ref, value_ref, out_ref):
    sel = sel_ref[...]
    pick = one_hot(picker(sel))
    live = column_of(sel.astype(F32)) >= 0.0
    key = jnp.where(live, dot(pick, key_ref[...]), FLAG).astype(BF)
    value = dot(pick, value_ref[...]).astype(BF)
    for copy in range(ROWS_Z):
        out_ref[copy, :, :HEAD_DIM] = key
        out_ref[copy, :, HEAD_DIM:] = value


def select_q_kernel(sel_ref, logit_ref, query_ref, cot_ref, q_ref, g_ref, c_ref, router_ref):
    mask = picker(sel_ref[...])
    pick = one_hot(mask)
    logit = jnp.sum(jnp.where(mask, logit_ref[...], 0.0), axis=1, keepdims=True)
    router = 1.0 / (1.0 + jnp.exp(-logit))
    router_ref[...] = jnp.broadcast_to(router, (SLOTS, SLOTS))
    for h in range(HEADS):
        cols = slice(h * HEAD_DIM, (h + 1) * HEAD_DIM)
        rows = slice(h * SLOTS, (h + 1) * SLOTS)
        q_ref[rows, :] = dot(pick, query_ref[:, cols]).astype(BF)
        cot = dot(pick, cot_ref[:, cols])
        c_ref[rows, :] = cot.astype(BF)
        g_ref[rows, :] = (router * cot).astype(BF)


def attention_kernel(pos_ref, kv0, kv1, kv2, kv3, q_ref, g_ref, c_ref,
                     att_ref, dq_ref, part0, part1, part2, part3, feat_ref,
                     lines, kvs, dkv_ref, s_ref, w_ref, at_ref, dqt_ref, top_ref, sum_ref, cen_ref, base_ref, sem):
    row = pos_ref[0]
    own = row * ROWS_Z + pos_ref[1]
    block = ROWS_Z * SLOTS
    copies = []
    for k, src in enumerate((kv0, kv1, kv2, kv3)):
        owner = lax.rem(row - k + ROWS_Y, ROWS_Y)
        start = pl.multiple_of(owner * block, block)
        copies.append(pltpu.make_async_copy(src, lines.at[pl.ds(start, block), :], sem.at[k]))
    for c in copies:
        c.start()
    at_ref[...] = jnp.zeros_like(at_ref)
    dqt_ref[...] = jnp.zeros_like(dqt_ref)
    top_ref[...] = jnp.full_like(top_ref, NEG)
    sum_ref[...] = jnp.zeros_like(sum_ref)
    for c in copies:
        c.wait()

    counts = []
    for s in range(SHARDS):
        flags = jnp.where(lines[s * SLOTS : (s + 1) * SLOTS, :HEAD_DIM].astype(F32) < 0.5 * FLAG, 1.0, 0.0)
        counts.append(jnp.max(jnp.sum(flags, axis=0, keepdims=True)).astype(jnp.int32))
    base = jnp.int32(0)
    for s in range(SHARDS):
        base_ref[s] = base
        at = pl.multiple_of(base, GROUP)
        kvs[pl.ds(at, SLOTS), :] = lines[s * SLOTS : (s + 1) * SLOTS, :]
        base = base + (counts[s] + (GROUP - 1)) // GROUP * GROUP
    base_ref[SHARDS] = base
    kvs[pl.ds(pl.multiple_of(base, GROUP), TILE), :] = jnp.zeros((TILE, 2 * HEAD_DIM), BF)
    query_id = base_ref[own]
    tiles = (base_ref[own + 1] + (TILE - 1)) // TILE

    def scores(t, carry):
        keys = kvs[pl.ds(pl.multiple_of(t * TILE, TILE), TILE), :HEAD_DIM]
        kid = t * TILE + lax.broadcasted_iota(jnp.int32, (TILE, SLOTS), 0)
        qid = query_id + lax.broadcasted_iota(jnp.int32, (TILE, SLOTS), 1)
        dead = jnp.broadcast_to(keys[:, :1].astype(F32), (TILE, SLOTS)) > 0.5 * FLAG
        bias = jnp.where((kid > qid) | dead, NEG, 0.0)
        bias = jnp.concatenate([bias] * (QCHUNK // SLOTS), axis=1)
        for c in range(LANES // QCHUNK):
            lanes = slice(c * QCHUNK, (c + 1) * QCHUNK)
            s = dot(keys, q_ref[lanes, :], NT) * (SCALE * LOG2E) + bias
            s_ref[pl.ds(pl.multiple_of(t * TILE, TILE), TILE), lanes] = s
            part = jnp.max(s.reshape(TILE // 8, 8, QCHUNK), axis=0)
            top_ref[:, lanes] = jnp.maximum(top_ref[:, lanes], part)
        return carry

    lax.fori_loop(0, tiles, scores, 0)
    top_ref[...] = jnp.broadcast_to(jnp.max(top_ref[...], axis=0, keepdims=True), top_ref.shape)

    def exponent(t, carry):
        rows = pl.ds(pl.multiple_of(t * TILE, TILE), TILE)
        for c in range(LANES // QCHUNK):
            lanes = slice(c * QCHUNK, (c + 1) * QCHUNK)
            e = jnp.exp2(s_ref[rows, lanes] - top_ref[:1, lanes])
            s_ref[rows, lanes] = e
            sum_ref[:, lanes] += jnp.sum(e.reshape(TILE // 8, 8, QCHUNK), axis=0)
        return carry

    lax.fori_loop(0, tiles, exponent, 0)
    total = jnp.sum(sum_ref[...], axis=0, keepdims=True)
    sum_ref[...] = jnp.broadcast_to(1.0 / total, sum_ref.shape)

    def forward(t, carry):
        rows = pl.ds(pl.multiple_of(t * TILE, TILE), TILE)
        value_t = jnp.transpose(kvs[rows, HEAD_DIM:])
        for c in range(LANES // QCHUNK):
            lanes = slice(c * QCHUNK, (c + 1) * QCHUNK)
            w = (s_ref[rows, lanes] * sum_ref[:1, lanes]).astype(BF)
            w_ref[rows, lanes] = w
            at_ref[:, lanes] += dot(value_t, w)
        dkv_ref[rows, HEAD_DIM:] = dot(w_ref[rows, :], g_ref[...]).astype(BF)
        return carry

    lax.fori_loop(0, tiles, forward, 0)

    feature = jnp.zeros((SLOTS, HEAD_DIM), F32)
    for h in range(HEADS):
        lanes = slice(h * HEAD_DIM, (h + 1) * HEAD_DIM)
        att_t = at_ref[:, lanes].astype(BF)
        att = jnp.transpose(att_t)
        att_ref[:, lanes] = att
        grad_t = jnp.transpose(g_ref[lanes, :])
        centre = jnp.sum(grad_t.astype(F32) * att_t.astype(F32), axis=0, keepdims=True)
        cen_ref[:, lanes] = jnp.broadcast_to(centre, (8, HEAD_DIM))
        feature += c_ref[lanes, :].astype(F32) * att.astype(F32)
    feature = jnp.broadcast_to(jnp.sum(feature, axis=1, keepdims=True), (SLOTS, SLOTS))
    feature = jnp.transpose(feature)[:8, :]
    for peer in range(8):
        feat_ref[peer] = feature

    def backward(t, carry):
        rows = pl.ds(pl.multiple_of(t * TILE, TILE), TILE)
        values = kvs[rows, HEAD_DIM:]
        key_t = jnp.transpose(kvs[rows, :HEAD_DIM])
        acc = jnp.zeros((TILE, HEAD_DIM), F32)
        for c in range(LANES // QCHUNK):
            lanes = slice(c * QCHUNK, (c + 1) * QCHUNK)
            slope = dot(values, g_ref[lanes, :], NT)
            ds = (w_ref[rows, lanes].astype(F32) * (slope - cen_ref[:1, lanes]) * SCALE).astype(BF)
            dqt_ref[:, lanes] += dot(key_t, ds)
            acc += dot(ds, q_ref[lanes, :])
        dkv_ref[rows, :HEAD_DIM] = acc.astype(BF)
        return carry

    lax.fori_loop(0, tiles, backward, 0)

    dkv_ref[pl.ds(pl.multiple_of(tiles * TILE, TILE), TILE), :] = jnp.zeros((TILE, 2 * HEAD_DIM), BF)
    for k, out in enumerate((part0, part1, part2, part3)):
        first = lax.rem(row + k, ROWS_Y) * ROWS_Z
        for z in range(ROWS_Z):
            at = pl.multiple_of(base_ref[first + z], GROUP)
            rows = dkv_ref[pl.ds(at, SLOTS), :]
            out[z * SLOTS : (z + 1) * SLOTS, :] = jnp.where(first + z <= own, rows, jnp.zeros_like(rows))
    for h in range(HEADS):
        lanes = slice(h * HEAD_DIM, (h + 1) * HEAD_DIM)
        dq_ref[:, lanes] = jnp.transpose(dqt_ref[:, lanes].astype(BF))


def place_q_kernel(sel_ref, router_ref, att_ref, dq_ref, mixed_ref, qgrad_ref):
    place = one_hot(placer(sel_ref[...]))
    router = router_ref[...]
    for h in range(HEADS):
        lanes = slice(h * HEAD_DIM, (h + 1) * HEAD_DIM)
        mix = (router * att_ref[:, lanes].astype(F32)).astype(BF)
        mixed_ref[:, lanes] = dot(place, mix).astype(BF)
        qgrad_ref[:, lanes] = dot(place, dq_ref[:, lanes]).astype(BF)


def add_rows_kernel(in0, in1, in2, in3, out_ref):
    total = in0[...].astype(F32)
    for ref in (in1, in2, in3):
        total += ref[...].astype(F32)
    total = total.astype(BF)
    for z in range(ROWS_Z):
        out_ref[z] = total[z * SLOTS : (z + 1) * SLOTS, :]


def place_kv_kernel(sel_ref, router_ref, feat_ref, part_ref, kgrad_ref, vgrad_ref, rgrad_ref):
    total = part_ref[0].astype(F32)
    for k in range(1, ROWS_Z):
        total += part_ref[k].astype(F32)
    placed = dot(one_hot(placer(sel_ref[...])), total.astype(BF)).astype(BF)
    kgrad_ref[...] = placed[:, :HEAD_DIM]
    vgrad_ref[...] = placed[:, HEAD_DIM:]
    feature = feat_ref[0]
    for k in range(1, 8):
        feature += feat_ref[k]
    router = router_ref[...]
    terms = router * (1.0 - router) * column_of(feature[:1, :])
    terms = jnp.concatenate([terms] * (TOK // SLOTS), axis=1)
    rgrad_ref[...] = jnp.sum(jnp.where(picker(sel_ref[...]), terms, 0.0), axis=0, keepdims=True)


def call(kernel, outs, args, scratch=(), specs=None, cost=None):
    return pl.pallas_call(
        kernel,
        out_shape=[jax.ShapeDtypeStruct(s, d) for s, d in outs],
        in_specs=specs or [pl.BlockSpec(memory_space=VMEM)] * len(args),
        out_specs=[pl.BlockSpec(memory_space=VMEM)] * len(outs),
        scratch_shapes=list(scratch),
        compiler_params=pltpu.CompilerParams(vmem_limit_bytes=LIMIT if scratch else 24 * 1024 * 1024),
        cost_estimate=pl.CostEstimate(flops=cost[0], bytes_accessed=cost[1], transcendentals=0),
    )(*args)


def shards(query_rows, key_rows, value_rows, cotangent, router_logits, selection):
    sel = selection.reshape(1, SLOTS)
    logits = router_logits.reshape(1, TOK)
    row = lax.axis_index("y")
    col = lax.axis_index("z")
    (own,) = call(select_kv_kernel, [((ROWS_Z, SLOTS, 2 * HEAD_DIM), BF)], (sel, key_rows, value_rows),
                  cost=(2 * SLOTS * TOK * 256, 1 << 20))
    line = lax.all_to_all(own, "z", 0, 0, tiled=True)
    q, g, c, router = call(
        select_q_kernel,
        [((LANES, HEAD_DIM), BF)] * 3 + [((SLOTS, SLOTS), F32)],
        (sel, logits, query_rows, cotangent),
        cost=(4 * SLOTS * TOK * LANES, 3 << 20))
    line = line.reshape(ROWS_Z * SLOTS, 2 * HEAD_DIM)
    lines = [line] + [
        lax.ppermute(line, "y", [(s, (s + k) % ROWS_Y) for s in range(ROWS_Y)]) for k in range(1, ROWS_Y)
    ]
    pos = jnp.stack([row, col]).astype(jnp.int32)
    specs = [pl.BlockSpec(memory_space=pltpu.SMEM)] + [pl.BlockSpec(memory_space=pl.ANY)] * 4
    specs += [pl.BlockSpec(memory_space=VMEM)] * 3
    block = ROWS_Z * SLOTS
    att, dq, *parts, feat = call(
        attention_kernel,
        [((SLOTS, LANES), BF)] * 2 + [((block, 2 * HEAD_DIM), BF)] * 4 + [((8, 8, SLOTS), F32)],
        (pos, *lines, q, g, c),
        scratch=[
            VMEM((KEYS, 2 * HEAD_DIM), BF), VMEM((PACKED + TILE, 2 * HEAD_DIM), BF),
            VMEM((PACKED + TILE, 2 * HEAD_DIM), BF), VMEM((PACKED, LANES), F32), VMEM((PACKED, LANES), BF),
            VMEM((HEAD_DIM, LANES), F32), VMEM((HEAD_DIM, LANES), F32),
            VMEM((8, LANES), F32), VMEM((8, LANES), F32), VMEM((8, LANES), F32),
            pltpu.SMEM((SHARDS + 1,), jnp.int32),
            pltpu.SemaphoreType.DMA((4,)),
        ],
        specs=specs,
        cost=(12 * PACKED * LANES * HEAD_DIM, 8 << 20))
    moved = [lax.ppermute(parts[k], "y", [(s, (s + k) % ROWS_Y) for s in range(ROWS_Y)]) for k in range(1, ROWS_Y)]
    feat = lax.all_to_all(feat, "mp", 0, 0, tiled=True)
    mixed, qgrad = call(place_q_kernel, [((TOK, LANES), BF)] * 2, (sel, router, att, dq),
                        cost=(4 * SLOTS * TOK * LANES, 3 << 20))
    (part,) = call(add_rows_kernel, [((ROWS_Z, SLOTS, 2 * HEAD_DIM), BF)], (parts[0], *moved),
                   cost=(1 << 20, 3 << 20))
    part = lax.all_to_all(part, "z", 0, 0, tiled=True)
    kgrad, vgrad, rgrad = call(
        place_kv_kernel,
        [((TOK, HEAD_DIM), BF)] * 2 + [((1, TOK), F32)],
        (sel, router, feat, part),
        cost=(2 * SLOTS * TOK * 256, 1 << 20))
    return mixed, qgrad, kgrad, vgrad, rgrad.reshape(TOK)


def solution(mesh):
    inner = Mesh(mesh.devices.reshape(ROWS_Y, ROWS_Z, 8), ("y", "z", "mp"))
    seq = ("y", "z")
    in_specs = (P(seq, "mp"), P(seq, "mp"), P(seq, "mp"), P(seq, "mp"), P(seq), P(seq))
    out_specs = (P(seq, "mp"), P(seq, "mp"), P(seq, "mp"), P(seq, "mp"), P(seq))
    return jax.shard_map(shards, mesh=inner, in_specs=in_specs, out_specs=out_specs, check_vma=False)
```

```python
import functools

import jax
import jax.numpy as jnp
from jax import lax
from jax.experimental import pallas as pl
from jax.experimental.pallas import tpu as pltpu
from jax.sharding import Mesh, PartitionSpec as P

HEAD_DIM = 128
SLOTS = 128
TOK = 512
HEADS = 8
ROWS_Y = 4
ROWS_Z = 8
LANES = HEADS * HEAD_DIM
TILE = 512
GROUP = 16
SHARDS = ROWS_Y * ROWS_Z
PACKED = 2560
QCHUNK = 256
FLAG = 64.0
NEG = -1e30
SCALE = HEAD_DIM ** (-0.5)
LOG2E = 1.4426950408889634
BF = jnp.bfloat16
F32 = jnp.float32
NT = (((1,), (1,)), ((), ()))
NN = (((1,), (0,)), ((), ()))
VMEM = pltpu.VMEM
LIMIT = 34 * 1024 * 1024


def dot(a, b, dims=NN):
    return lax.dot_general(a, b, dims, preferred_element_type=F32)


def column_of(row):
    return jnp.transpose(jnp.broadcast_to(row, (SLOTS, SLOTS)))


def picker(sel_row):
    col = column_of(sel_row.astype(F32))
    lane = lax.broadcasted_iota(jnp.int32, (SLOTS, SLOTS), 1).astype(F32)
    return jnp.concatenate([col == lane + float(c * SLOTS) for c in range(TOK // SLOTS)], axis=1)


def placer(sel_row):
    token = lax.broadcasted_iota(jnp.int32, (TOK, SLOTS), 0)
    return jnp.broadcast_to(sel_row, (TOK, SLOTS)) == token


def one_hot(mask):
    return jnp.where(mask, 1.0, 0.0).astype(BF)


def select_kv_kernel(sel_hbm, key_hbm, value_hbm, out_ref, sel_ref, key_ref, value_ref, sem):
    copies = [
        pltpu.make_async_copy(src, dst, sem.at[i])
        for i, (src, dst) in enumerate(((sel_hbm, sel_ref), (key_hbm, key_ref), (value_hbm, value_ref)))
    ]
    for c in copies:
        c.start()
    copies[0].wait()
    sel = sel_ref[...]
    pick = one_hot(picker(sel))
    live = column_of(sel.astype(F32)) >= 0.0
    copies[1].wait()
    key = jnp.where(live, dot(pick, key_ref[...]), FLAG).astype(BF)
    copies[2].wait()
    value = dot(pick, value_ref[...]).astype(BF)
    for copy in range(ROWS_Z):
        out_ref[copy, :, :HEAD_DIM] = key
        out_ref[copy, :, HEAD_DIM:] = value


def select_q_kernel(sel_ref, logit_ref, query_ref, cot_ref, q_ref, g_ref, c_ref, router_ref):
    mask = picker(sel_ref[...])
    pick = one_hot(mask)
    logit = jnp.sum(jnp.where(mask, logit_ref[...], 0.0), axis=1, keepdims=True)
    router = 1.0 / (1.0 + jnp.exp(-logit))
    router_ref[...] = jnp.broadcast_to(router, (SLOTS, SLOTS))
    for h in range(HEADS):
        cols = slice(h * HEAD_DIM, (h + 1) * HEAD_DIM)
        rows = slice(h * SLOTS, (h + 1) * SLOTS)
        q_ref[rows, :] = dot(pick, query_ref[:, cols]).astype(BF)
        cot = dot(pick, cot_ref[:, cols])
        c_ref[rows, :] = cot.astype(BF)
        g_ref[rows, :] = (router * cot).astype(BF)


def attention_kernel(pos_ref, kv0, kv1, kv2, kv3, q_ref, g_ref, c_ref,
                     att_ref, dq_ref, part0, part1, part2, part3, feat_ref,
                     kvs, dkv_ref, s_ref, w_ref, at_ref, dqt_ref, top_ref, sum_ref, cen_ref, tops_ref, base_ref):
    row = pos_ref[0]
    col = pos_ref[1]
    own = row * ROWS_Z + col
    at_ref[...] = jnp.zeros_like(at_ref)
    dqt_ref[...] = jnp.zeros_like(dqt_ref)
    top_ref[...] = jnp.full_like(top_ref, NEG)
    sum_ref[...] = jnp.zeros_like(sum_ref)

    lines = (kv0, kv1, kv2, kv3)
    counts = {}
    for k in reversed(range(ROWS_Y)):
        for z in range(ROWS_Z):
            flags = lines[k][z * SLOTS : (z + 1) * SLOTS, :HEAD_DIM].astype(F32) < 0.5 * FLAG
            live = jnp.sum(jnp.where(flags, 1.0, 0.0), axis=0, keepdims=True)
            count = jnp.max(live).astype(jnp.int32)
            past = z <= col if k == 0 else k <= row
            counts[k, z] = jnp.where(past, (count + (GROUP - 1)) // GROUP * GROUP, 0)
    base = jnp.int32(0)
    for k in reversed(range(ROWS_Y)):
        first = lax.rem(row - k + ROWS_Y, ROWS_Y) * ROWS_Z
        for z in range(ROWS_Z):
            base_ref[first + z] = base
            kvs[pl.ds(pl.multiple_of(base, GROUP), SLOTS), :] = lines[k][z * SLOTS : (z + 1) * SLOTS, :]
            base = base + counts[k, z]
    kvs[pl.ds(pl.multiple_of(base, GROUP), TILE), :] = jnp.zeros((TILE, 2 * HEAD_DIM), BF)
    query_id = base_ref[own]
    tiles = (base + (TILE - 1)) // TILE

    def scores(t, carry):
        rows = pl.ds(pl.multiple_of(t * TILE, TILE), TILE)
        keys = kvs[rows, :HEAD_DIM]
        kid = t * TILE + lax.broadcasted_iota(jnp.int32, (TILE, SLOTS), 0)
        qid = query_id + lax.broadcasted_iota(jnp.int32, (TILE, SLOTS), 1)
        dead = jnp.broadcast_to(keys[:, :1].astype(F32), (TILE, SLOTS)) > 0.5 * FLAG
        bias = jnp.where((kid > qid) | dead, NEG, 0.0)
        bias = jnp.concatenate([bias] * (QCHUNK // SLOTS), axis=1)
        for c in range(LANES // QCHUNK):
            lanes = slice(c * QCHUNK, (c + 1) * QCHUNK)
            s = dot(keys, q_ref[lanes, :], NT) * (SCALE * LOG2E) + bias
            s = s.reshape(TILE // 8, 8, QCHUNK)
            old = top_ref[:, lanes]
            new = jnp.maximum(old, jnp.max(s, axis=0))
            e = jnp.exp2(s - new[None])
            top_ref[:, lanes] = new
            tops_ref[t, :, lanes] = new
            sum_ref[:, lanes] = sum_ref[:, lanes] * jnp.exp2(old - new) + jnp.sum(e, axis=0)
            s_ref[rows, lanes] = e.reshape(TILE, QCHUNK)
        return carry

    lax.fori_loop(0, tiles, scores, 0)
    top = jnp.max(top_ref[...], axis=0, keepdims=True)
    total = jnp.sum(sum_ref[...] * jnp.exp2(top_ref[...] - top), axis=0, keepdims=True)
    top_ref[...] = jnp.broadcast_to(top, top_ref.shape)
    sum_ref[...] = jnp.broadcast_to(1.0 / total, sum_ref.shape)

    def forward(t, carry):
        rows = pl.ds(pl.multiple_of(t * TILE, TILE), TILE)
        values = kvs[rows, HEAD_DIM:]
        value_t = jnp.transpose(values)
        acc = jnp.zeros((TILE, HEAD_DIM), F32)
        for c in range(LANES // QCHUNK):
            lanes = slice(c * QCHUNK, (c + 1) * QCHUNK)
            factor = jnp.exp2(tops_ref[t, :, lanes] - top_ref[:, lanes]) * sum_ref[:, lanes]
            w = s_ref[rows, lanes].reshape(TILE // 8, 8, QCHUNK) * factor[None]
            w = w.reshape(TILE, QCHUNK).astype(BF)
            w_ref[rows, lanes] = w
            at_ref[:, lanes] += dot(value_t, w)
            acc += dot(w, g_ref[lanes, :])
            s_ref[rows, lanes] = dot(values, g_ref[lanes, :], NT)
        dkv_ref[rows, HEAD_DIM:] = acc.astype(BF)
        return carry

    lax.fori_loop(0, tiles, forward, 0)

    feature = jnp.zeros((SLOTS, HEAD_DIM), F32)
    for h in range(HEADS):
        lanes = slice(h * HEAD_DIM, (h + 1) * HEAD_DIM)
        att_t = at_ref[:, lanes].astype(BF)
        att = jnp.transpose(att_t)
        att_ref[:, lanes] = att
        grad_t = jnp.transpose(g_ref[lanes, :])
        centre = jnp.sum(grad_t.astype(F32) * att_t.astype(F32), axis=0, keepdims=True)
        cen_ref[:, lanes] = jnp.broadcast_to(centre, (8, HEAD_DIM))
        feature += c_ref[lanes, :].astype(F32) * att.astype(F32)
    feature = jnp.broadcast_to(jnp.sum(feature, axis=1, keepdims=True), (SLOTS, SLOTS))
    feature = jnp.transpose(feature)[:8, :]
    for peer in range(8):
        feat_ref[peer] = feature

    def backward(t, carry):
        rows = pl.ds(pl.multiple_of(t * TILE, TILE), TILE)
        key_t = jnp.transpose(kvs[rows, :HEAD_DIM])
        acc = jnp.zeros((TILE, HEAD_DIM), F32)
        for c in range(LANES // QCHUNK):
            lanes = slice(c * QCHUNK, (c + 1) * QCHUNK)
            slope = s_ref[rows, lanes].reshape(TILE // 8, 8, QCHUNK)
            w = w_ref[rows, lanes].astype(F32).reshape(TILE // 8, 8, QCHUNK)
            ds = (w * (slope - cen_ref[:, lanes][None]) * SCALE).reshape(TILE, QCHUNK).astype(BF)
            dqt_ref[:, lanes] += dot(key_t, ds)
            acc += dot(ds, q_ref[lanes, :])
        dkv_ref[rows, :HEAD_DIM] = acc.astype(BF)
        return carry

    lax.fori_loop(0, tiles, backward, 0)

    dkv_ref[pl.ds(pl.multiple_of(tiles * TILE, TILE), TILE), :] = jnp.zeros((TILE, 2 * HEAD_DIM), BF)
    for k, out in enumerate((part0, part1, part2, part3)):
        first = lax.rem(row + k, ROWS_Y) * ROWS_Z
        for z in range(ROWS_Z):
            at = pl.multiple_of(base_ref[first + z], GROUP)
            rows = dkv_ref[pl.ds(at, SLOTS), :]
            out[z * SLOTS : (z + 1) * SLOTS, :] = jnp.where(first + z <= own, rows, jnp.zeros_like(rows))
    for h in range(HEADS):
        lanes = slice(h * HEAD_DIM, (h + 1) * HEAD_DIM)
        dq_ref[:, lanes] = jnp.transpose(dqt_ref[:, lanes].astype(BF))


def place_q_kernel(sel_ref, router_ref, att_ref, dq_ref, mixed_ref, qgrad_ref):
    place = one_hot(placer(sel_ref[...]))
    router = router_ref[...]
    for h in range(HEADS):
        lanes = slice(h * HEAD_DIM, (h + 1) * HEAD_DIM)
        mix = (router * att_ref[:, lanes].astype(F32)).astype(BF)
        mixed_ref[:, lanes] = dot(place, mix).astype(BF)
        qgrad_ref[:, lanes] = dot(place, dq_ref[:, lanes]).astype(BF)


def add_rows_kernel(in0, in1, in2, in3, out_ref):
    total = in0[...].astype(F32)
    for ref in (in1, in2, in3):
        total += ref[...].astype(F32)
    total = total.astype(BF)
    for z in range(ROWS_Z):
        out_ref[z] = total[z * SLOTS : (z + 1) * SLOTS, :]


def place_kv_kernel(sel_ref, router_ref, feat_ref, part_ref, kgrad_ref, vgrad_ref, rgrad_ref):
    total = part_ref[0].astype(F32)
    for k in range(1, ROWS_Z):
        total += part_ref[k].astype(F32)
    placed = dot(one_hot(placer(sel_ref[...])), total.astype(BF)).astype(BF)
    kgrad_ref[...] = placed[:, :HEAD_DIM]
    vgrad_ref[...] = placed[:, HEAD_DIM:]
    feature = feat_ref[0]
    for k in range(1, 8):
        feature += feat_ref[k]
    router = router_ref[...]
    terms = router * (1.0 - router) * column_of(feature[:1, :])
    terms = jnp.concatenate([terms] * (TOK // SLOTS), axis=1)
    rgrad_ref[...] = jnp.sum(jnp.where(picker(sel_ref[...]), terms, 0.0), axis=0, keepdims=True)


def call(kernel, outs, args, scratch=(), specs=None, cost=None, limit=12 * 1024 * 1024):
    return pl.pallas_call(
        kernel,
        out_shape=[jax.ShapeDtypeStruct(s, d) for s, d in outs],
        in_specs=specs or [pl.BlockSpec(memory_space=VMEM)] * len(args),
        out_specs=[pl.BlockSpec(memory_space=VMEM)] * len(outs),
        scratch_shapes=list(scratch),
        compiler_params=pltpu.CompilerParams(vmem_limit_bytes=limit),
        cost_estimate=pl.CostEstimate(flops=cost[0], bytes_accessed=cost[1], transcendentals=0),
    )(*args)


def attend(pos, kv0, kv1, kv2, kv3, q, g, c):
    specs = [pl.BlockSpec(memory_space=pltpu.SMEM)] + [pl.BlockSpec(memory_space=VMEM)] * 7
    block = ROWS_Z * SLOTS
    return call(
        attention_kernel,
        [((SLOTS, LANES), BF)] * 2 + [((block, 2 * HEAD_DIM), BF)] * 4 + [((8, 8, SLOTS), F32)],
        (pos, kv0, kv1, kv2, kv3, q, g, c),
        scratch=[
            VMEM((PACKED + TILE, 2 * HEAD_DIM), BF),
            VMEM((PACKED + TILE, 2 * HEAD_DIM), BF), VMEM((PACKED, LANES), F32), VMEM((PACKED, LANES), BF),
            VMEM((HEAD_DIM, LANES), F32), VMEM((HEAD_DIM, LANES), F32),
            VMEM((8, LANES), F32), VMEM((8, LANES), F32), VMEM((8, LANES), F32),
            VMEM((PACKED // TILE, 8, LANES), F32),
            pltpu.SMEM((SHARDS,), jnp.int32),
        ],
        specs=specs,
        cost=(12 * PACKED * LANES * HEAD_DIM, 8 << 20),
        limit=LIMIT)


def shards(query_rows, key_rows, value_rows, cotangent, router_logits, selection):
    sel = selection.reshape(1, SLOTS)
    logits = router_logits.reshape(1, TOK)
    row = lax.axis_index("y")
    col = lax.axis_index("z")
    (own,) = call(select_kv_kernel, [((ROWS_Z, SLOTS, 2 * HEAD_DIM), BF)], (sel, key_rows, value_rows),
                  scratch=[VMEM((1, SLOTS), jnp.int32), VMEM((TOK, HEAD_DIM), BF), VMEM((TOK, HEAD_DIM), BF),
                           pltpu.SemaphoreType.DMA((3,))],
                  specs=[pl.BlockSpec(memory_space=pltpu.HBM)] * 3,
                  cost=(2 * SLOTS * TOK * 256, 1 << 20), limit=60 * 1024 * 1024)
    line = lax.all_to_all(own, "z", 0, 0, tiled=True)
    q, g, c, router = call(
        select_q_kernel,
        [((LANES, HEAD_DIM), BF)] * 3 + [((SLOTS, SLOTS), F32)],
        (sel, logits, query_rows, cotangent),
        cost=(4 * SLOTS * TOK * LANES, 3 << 20))
    line = line.reshape(ROWS_Z * SLOTS, 2 * HEAD_DIM)
    lines = [line] + [
        lax.ppermute(line, "y", [(s, (s + k) % ROWS_Y) for s in range(ROWS_Y)]) for k in range(1, ROWS_Y)
    ]
    pos = jnp.stack([row, col]).astype(jnp.int32)
    att, dq, *parts, feat = attend(pos, *lines, q, g, c)
    moved = [lax.ppermute(parts[k], "y", [(s, (s + k) % ROWS_Y) for s in range(ROWS_Y)]) for k in range(1, ROWS_Y)]
    feat = lax.all_to_all(feat, "mp", 0, 0, tiled=True)
    mixed, qgrad = call(place_q_kernel, [((TOK, LANES), BF)] * 2, (sel, router, att, dq),
                        cost=(4 * SLOTS * TOK * LANES, 3 << 20))
    (part,) = call(add_rows_kernel, [((ROWS_Z, SLOTS, 2 * HEAD_DIM), BF)], (parts[0], *moved),
                   cost=(1 << 20, 3 << 20))
    part = lax.all_to_all(part, "z", 0, 0, tiled=True)
    kgrad, vgrad, rgrad = call(
        place_kv_kernel,
        [((TOK, HEAD_DIM), BF)] * 2 + [((1, TOK), F32)],
        (sel, router, feat, part),
        cost=(2 * SLOTS * TOK * 256, 1 << 20))
    return mixed, qgrad, kgrad, vgrad, rgrad.reshape(TOK)


def solution(mesh):
    inner = Mesh(mesh.devices.reshape(ROWS_Y, ROWS_Z, 8), ("y", "z", "mp"))
    seq = ("y", "z")
    in_specs = (P(seq, "mp"), P(seq, "mp"), P(seq, "mp"), P(seq, "mp"), P(seq), P(seq))
    out_specs = (P(seq, "mp"), P(seq, "mp"), P(seq, "mp"), P(seq, "mp"), P(seq))
    return jax.shard_map(shards, mesh=inner, in_specs=in_specs, out_specs=out_specs, check_vma=False)
```

```python
import functools

import jax
import jax.numpy as jnp
from jax import lax
from jax.experimental import pallas as pl
from jax.experimental.pallas import tpu as pltpu
from jax.sharding import Mesh, PartitionSpec as P

HEAD_DIM = 128
SLOTS = 128
TOK = 512
HEADS = 8
ROWS_Y = 4
ROWS_Z = 8
LANES = HEADS * HEAD_DIM
TILE = 512
GROUP = 16
SHARDS = ROWS_Y * ROWS_Z
PACKED = 2560
QCHUNK = 256
FAR = (2, 3, 6, 5, 4)
NEAR = (0, 1, 7)
FLAG = 64.0
NEG = -1e30
SCALE = HEAD_DIM ** (-0.5)
LOG2E = 1.4426950408889634
BF = jnp.bfloat16
F32 = jnp.float32
NT = (((1,), (1,)), ((), ()))
NN = (((1,), (0,)), ((), ()))
VMEM = pltpu.VMEM
LIMIT = 34 * 1024 * 1024


def dot(a, b, dims=NN):
    return lax.dot_general(a, b, dims, preferred_element_type=F32)


def column_of(row):
    return jnp.transpose(jnp.broadcast_to(row, (SLOTS, SLOTS)))


def picker(sel_row):
    col = column_of(sel_row.astype(F32))
    lane = lax.broadcasted_iota(jnp.int32, (SLOTS, SLOTS), 1).astype(F32)
    return jnp.concatenate([col == lane + float(c * SLOTS) for c in range(TOK // SLOTS)], axis=1)


def placer(sel_row):
    token = lax.broadcasted_iota(jnp.int32, (TOK, SLOTS), 0)
    return jnp.broadcast_to(sel_row, (TOK, SLOTS)) == token


def one_hot(mask):
    return jnp.where(mask, 1.0, 0.0).astype(BF)


def select_kv_kernel(sel_hbm, key_hbm, value_hbm, out_ref, sel_ref, key_ref, value_ref, sem):
    copies = [
        pltpu.make_async_copy(src, dst, sem.at[i])
        for i, (src, dst) in enumerate(((sel_hbm, sel_ref), (key_hbm, key_ref), (value_hbm, value_ref)))
    ]
    for c in copies:
        c.start()
    copies[0].wait()
    sel = sel_ref[...]
    pick = one_hot(picker(sel))
    live = column_of(sel.astype(F32)) >= 0.0
    copies[1].wait()
    key = jnp.where(live, dot(pick, key_ref[...]), FLAG).astype(BF)
    copies[2].wait()
    value = dot(pick, value_ref[...]).astype(BF)
    out_ref[:, :HEAD_DIM] = key
    out_ref[:, HEAD_DIM:] = value


def select_q_kernel(sel_ref, logit_ref, query_ref, cot_ref, q_ref, g_ref, c_ref, router_ref):
    mask = picker(sel_ref[...])
    pick = one_hot(mask)
    logit = jnp.sum(jnp.where(mask, logit_ref[...], 0.0), axis=1, keepdims=True)
    router = 1.0 / (1.0 + jnp.exp(-logit))
    router_ref[...] = jnp.broadcast_to(router, (SLOTS, SLOTS))
    for h in range(HEADS):
        cols = slice(h * HEAD_DIM, (h + 1) * HEAD_DIM)
        rows = slice(h * SLOTS, (h + 1) * SLOTS)
        q_ref[rows, :] = dot(pick, query_ref[:, cols]).astype(BF)
        cot = dot(pick, cot_ref[:, cols])
        c_ref[rows, :] = cot.astype(BF)
        g_ref[rows, :] = (router * cot).astype(BF)


def attention_kernel(pos_ref, ev0, ev1, ev2, ev3, od0, od1, od2, od3, q_ref, g_ref, c_ref,
                     att_ref, dq_ref, far0, far1, far2, far3, near0, near1, near2, near3, feat_ref,
                     kvs, dkv_ref, s_ref, w_ref, at_ref, dqt_ref, top_ref, sum_ref, cen_ref, tops_ref, base_ref):
    row = pos_ref[0]
    col = pos_ref[1]
    own = row * ROWS_Z + col
    at_ref[...] = jnp.zeros_like(at_ref)
    dqt_ref[...] = jnp.zeros_like(dqt_ref)
    top_ref[...] = jnp.full_like(top_ref, NEG)
    sum_ref[...] = jnp.zeros_like(sum_ref)

    evens, odds = (ev0, ev1, ev2, ev3), (od0, od1, od2, od3)

    def shard_rows(k, z):
        step = lax.rem(z - col + ROWS_Z, ROWS_Z)
        even = pl.multiple_of(lax.rem(step + 2, ROWS_Z) // 2 * SLOTS, SLOTS)
        odd = pl.multiple_of(step // 2 * SLOTS, SLOTS)
        return jnp.where(lax.rem(step, 2) == 0, evens[k][pl.ds(even, SLOTS), :], odds[k][pl.ds(odd, SLOTS), :])

    counts = {}
    for k in reversed(range(ROWS_Y)):
        for z in range(ROWS_Z):
            flags = shard_rows(k, z)[:, :HEAD_DIM].astype(F32) < 0.5 * FLAG
            live = jnp.sum(jnp.where(flags, 1.0, 0.0), axis=0, keepdims=True)
            count = jnp.max(live).astype(jnp.int32)
            past = z <= col if k == 0 else k <= row
            counts[k, z] = jnp.where(past, (count + (GROUP - 1)) // GROUP * GROUP, 0)
    base = jnp.int32(0)
    for k in reversed(range(ROWS_Y)):
        first = lax.rem(row - k + ROWS_Y, ROWS_Y) * ROWS_Z
        for z in range(ROWS_Z):
            base_ref[first + z] = base
            kvs[pl.ds(pl.multiple_of(base, GROUP), SLOTS), :] = shard_rows(k, z)
            base = base + counts[k, z]
    kvs[pl.ds(pl.multiple_of(base, GROUP), TILE), :] = jnp.zeros((TILE, 2 * HEAD_DIM), BF)
    query_id = base_ref[own]
    tiles = (base + (TILE - 1)) // TILE

    def scores(t, carry):
        rows = pl.ds(pl.multiple_of(t * TILE, TILE), TILE)
        keys = kvs[rows, :HEAD_DIM]
        kid = t * TILE + lax.broadcasted_iota(jnp.int32, (TILE, SLOTS), 0)
        qid = query_id + lax.broadcasted_iota(jnp.int32, (TILE, SLOTS), 1)
        dead = jnp.broadcast_to(keys[:, :1].astype(F32), (TILE, SLOTS)) > 0.5 * FLAG
        bias = jnp.where((kid > qid) | dead, NEG, 0.0)
        bias = jnp.concatenate([bias] * (QCHUNK // SLOTS), axis=1)
        for c in range(LANES // QCHUNK):
            lanes = slice(c * QCHUNK, (c + 1) * QCHUNK)
            s = dot(keys, q_ref[lanes, :], NT) * (SCALE * LOG2E) + bias
            s = s.reshape(TILE // 8, 8, QCHUNK)
            old = top_ref[:, lanes]
            new = jnp.maximum(old, jnp.max(s, axis=0))
            e = jnp.exp2(s - new[None])
            top_ref[:, lanes] = new
            tops_ref[t, :, lanes] = new
            sum_ref[:, lanes] = sum_ref[:, lanes] * jnp.exp2(old - new) + jnp.sum(e, axis=0)
            s_ref[rows, lanes] = e.reshape(TILE, QCHUNK)
        return carry

    lax.fori_loop(0, tiles, scores, 0)
    top = jnp.max(top_ref[...], axis=0, keepdims=True)
    total = jnp.sum(sum_ref[...] * jnp.exp2(top_ref[...] - top), axis=0, keepdims=True)
    top_ref[...] = jnp.broadcast_to(top, top_ref.shape)
    sum_ref[...] = jnp.broadcast_to(1.0 / total, sum_ref.shape)

    def forward(t, carry):
        rows = pl.ds(pl.multiple_of(t * TILE, TILE), TILE)
        values = kvs[rows, HEAD_DIM:]
        value_t = jnp.transpose(values)
        acc = jnp.zeros((TILE, HEAD_DIM), F32)
        for c in range(LANES // QCHUNK):
            lanes = slice(c * QCHUNK, (c + 1) * QCHUNK)
            factor = jnp.exp2(tops_ref[t, :, lanes] - top_ref[:, lanes]) * sum_ref[:, lanes]
            w = s_ref[rows, lanes].reshape(TILE // 8, 8, QCHUNK) * factor[None]
            w = w.reshape(TILE, QCHUNK).astype(BF)
            w_ref[rows, lanes] = w
            at_ref[:, lanes] += dot(value_t, w)
            acc += dot(w, g_ref[lanes, :])
            s_ref[rows, lanes] = dot(values, g_ref[lanes, :], NT)
        dkv_ref[rows, HEAD_DIM:] = acc.astype(BF)
        return carry

    lax.fori_loop(0, tiles, forward, 0)

    feature = jnp.zeros((SLOTS, HEAD_DIM), F32)
    for h in range(HEADS):
        lanes = slice(h * HEAD_DIM, (h + 1) * HEAD_DIM)
        att_t = at_ref[:, lanes].astype(BF)
        att = jnp.transpose(att_t)
        att_ref[:, lanes] = att
        grad_t = jnp.transpose(g_ref[lanes, :])
        centre = jnp.sum(grad_t.astype(F32) * att_t.astype(F32), axis=0, keepdims=True)
        cen_ref[:, lanes] = jnp.broadcast_to(centre, (8, HEAD_DIM))
        feature += c_ref[lanes, :].astype(F32) * att.astype(F32)
    feature = jnp.broadcast_to(jnp.sum(feature, axis=1, keepdims=True), (SLOTS, SLOTS))
    feature = jnp.transpose(feature)[:8, :]
    for peer in range(8):
        feat_ref[peer] = feature

    def backward(t, carry):
        rows = pl.ds(pl.multiple_of(t * TILE, TILE), TILE)
        key_t = jnp.transpose(kvs[rows, :HEAD_DIM])
        acc = jnp.zeros((TILE, HEAD_DIM), F32)
        for c in range(LANES // QCHUNK):
            lanes = slice(c * QCHUNK, (c + 1) * QCHUNK)
            slope = s_ref[rows, lanes].reshape(TILE // 8, 8, QCHUNK)
            w = w_ref[rows, lanes].astype(F32).reshape(TILE // 8, 8, QCHUNK)
            ds = (w * (slope - cen_ref[:, lanes][None]) * SCALE).reshape(TILE, QCHUNK).astype(BF)
            dqt_ref[:, lanes] += dot(key_t, ds)
            acc += dot(ds, q_ref[lanes, :])
        dkv_ref[rows, :HEAD_DIM] = acc.astype(BF)
        return carry

    lax.fori_loop(0, tiles, backward, 0)

    dkv_ref[pl.ds(pl.multiple_of(tiles * TILE, TILE), TILE), :] = jnp.zeros((TILE, 2 * HEAD_DIM), BF)
    for k, (far, near) in enumerate(((far0, near0), (far1, near1), (far2, near2), (far3, near3))):
        first = lax.rem(row + k, ROWS_Y) * ROWS_Z
        for out, steps in ((far, FAR), (near, NEAR)):
            for i, step in enumerate(steps):
                shard = first + lax.rem(col + step, ROWS_Z)
                rows = dkv_ref[pl.ds(pl.multiple_of(base_ref[shard], GROUP), SLOTS), :]
                out[i * SLOTS : (i + 1) * SLOTS, :] = jnp.where(shard <= own, rows, jnp.zeros_like(rows))
    for h in range(HEADS):
        lanes = slice(h * HEAD_DIM, (h + 1) * HEAD_DIM)
        dq_ref[:, lanes] = jnp.transpose(dqt_ref[:, lanes].astype(BF))


def place_q_kernel(sel_ref, router_ref, att_ref, dq_ref, mixed_ref, qgrad_ref):
    place = one_hot(placer(sel_ref[...]))
    router = router_ref[...]
    for h in range(HEADS):
        lanes = slice(h * HEAD_DIM, (h + 1) * HEAD_DIM)
        mix = (router * att_ref[:, lanes].astype(F32)).astype(BF)
        mixed_ref[:, lanes] = dot(place, mix).astype(BF)
        qgrad_ref[:, lanes] = dot(place, dq_ref[:, lanes]).astype(BF)


def sum_of(*refs):
    total = refs[0][...].astype(F32)
    for ref in refs[1:]:
        total += ref[...].astype(F32)
    return total


def add_far_kernel(in0, in1, in2, in3, up_ref, down_ref, across_ref):
    total = sum_of(in0, in1, in2, in3).astype(BF)
    up_ref[...] = total[: 2 * SLOTS]
    down_ref[...] = total[2 * SLOTS : 4 * SLOTS]
    across_ref[...] = total[4 * SLOTS :]


def add_near_kernel(in0, in1, in2, in3, up_ref, down_ref, across_ref, own_ref, next_ref, prev_ref):
    total = sum_of(in0, in1, in2, in3)
    up = up_ref[...].astype(F32)
    down = down_ref[...].astype(F32)
    own_ref[...] = (total[:SLOTS] + up[:SLOTS] + down[:SLOTS] + across_ref[...].astype(F32)).astype(BF)
    next_ref[...] = (total[SLOTS : 2 * SLOTS] + up[SLOTS:]).astype(BF)
    prev_ref[...] = (total[2 * SLOTS :] + down[SLOTS:]).astype(BF)


def place_kv_kernel(sel_ref, router_ref, feat_ref, own_ref, prev_ref, next_ref, kgrad_ref, vgrad_ref, rgrad_ref):
    total = sum_of(own_ref, prev_ref, next_ref)
    placed = dot(one_hot(placer(sel_ref[...])), total.astype(BF)).astype(BF)
    kgrad_ref[...] = placed[:, :HEAD_DIM]
    vgrad_ref[...] = placed[:, HEAD_DIM:]
    feature = feat_ref[0]
    for k in range(1, 8):
        feature += feat_ref[k]
    router = router_ref[...]
    terms = router * (1.0 - router) * column_of(feature[:1, :])
    terms = jnp.concatenate([terms] * (TOK // SLOTS), axis=1)
    rgrad_ref[...] = jnp.sum(jnp.where(picker(sel_ref[...]), terms, 0.0), axis=0, keepdims=True)


def call(kernel, outs, args, scratch=(), specs=None, cost=None, limit=12 * 1024 * 1024):
    return pl.pallas_call(
        kernel,
        out_shape=[jax.ShapeDtypeStruct(s, d) for s, d in outs],
        in_specs=specs or [pl.BlockSpec(memory_space=VMEM)] * len(args),
        out_specs=[pl.BlockSpec(memory_space=VMEM)] * len(outs),
        scratch_shapes=list(scratch),
        compiler_params=pltpu.CompilerParams(vmem_limit_bytes=limit),
        cost_estimate=pl.CostEstimate(flops=cost[0], bytes_accessed=cost[1], transcendentals=0),
    )(*args)


def along_z(rows, step):
    return lax.ppermute(rows, "z", [(s, (s + step) % ROWS_Z) for s in range(ROWS_Z)])


def along_y(rows, step):
    return lax.ppermute(rows, "y", [(s, (s + step) % ROWS_Y) for s in range(ROWS_Y)])


def attend(pos, ev0, ev1, ev2, ev3, od0, od1, od2, od3, q, g, c):
    specs = [pl.BlockSpec(memory_space=pltpu.SMEM)] + [pl.BlockSpec(memory_space=VMEM)] * 11
    return call(
        attention_kernel,
        [((SLOTS, LANES), BF)] * 2 + [((len(FAR) * SLOTS, 2 * HEAD_DIM), BF)] * 4
        + [((len(NEAR) * SLOTS, 2 * HEAD_DIM), BF)] * 4 + [((8, 8, SLOTS), F32)],
        (pos, ev0, ev1, ev2, ev3, od0, od1, od2, od3, q, g, c),
        scratch=[
            VMEM((PACKED + TILE, 2 * HEAD_DIM), BF),
            VMEM((PACKED + TILE, 2 * HEAD_DIM), BF), VMEM((PACKED, LANES), F32), VMEM((PACKED, LANES), BF),
            VMEM((HEAD_DIM, LANES), F32), VMEM((HEAD_DIM, LANES), F32),
            VMEM((8, LANES), F32), VMEM((8, LANES), F32), VMEM((8, LANES), F32),
            VMEM((PACKED // TILE, 8, LANES), F32),
            pltpu.SMEM((SHARDS,), jnp.int32),
        ],
        specs=specs,
        cost=(12 * PACKED * LANES * HEAD_DIM, 8 << 20),
        limit=LIMIT)


def shards(query_rows, key_rows, value_rows, cotangent, router_logits, selection):
    sel = selection.reshape(1, SLOTS)
    logits = router_logits.reshape(1, TOK)
    row = lax.axis_index("y")
    col = lax.axis_index("z")
    (own,) = call(select_kv_kernel, [((SLOTS, 2 * HEAD_DIM), BF)], (sel, key_rows, value_rows),
                  scratch=[VMEM((1, SLOTS), jnp.int32), VMEM((TOK, HEAD_DIM), BF), VMEM((TOK, HEAD_DIM), BF),
                           pltpu.SemaphoreType.DMA((3,))],
                  specs=[pl.BlockSpec(memory_space=pltpu.HBM)] * 3,
                  cost=(2 * SLOTS * TOK * 256, 1 << 20), limit=60 * 1024 * 1024)
    across, up, down = along_z(own, 4), along_z(own, 2), along_z(own, 6)
    even = jnp.concatenate([up, own, down, across], axis=0)
    near, far = along_z(even[SLOTS : 3 * SLOTS], 7), along_z(even[: 2 * SLOTS], 1)
    evens = [even] + [along_y(even, k) for k in range(1, ROWS_Y)]
    odd = jnp.concatenate([near, far], axis=0)
    odds = [odd] + [along_y(odd, k) for k in range(1, ROWS_Y)]
    q, g, c, router = call(
        select_q_kernel,
        [((LANES, HEAD_DIM), BF)] * 3 + [((SLOTS, SLOTS), F32)],
        (sel, logits, query_rows, cotangent),
        cost=(4 * SLOTS * TOK * LANES, 3 << 20))
    pos = jnp.stack([row, col]).astype(jnp.int32)
    att, dq, *parts, feat = attend(pos, *evens, *odds, q, g, c)
    far = [parts[0]] + [along_y(parts[k], k) for k in range(1, ROWS_Y)]
    near = [parts[4]] + [along_y(parts[4 + k], k) for k in range(1, ROWS_Y)]
    feat = lax.all_to_all(feat, "mp", 0, 0, tiled=True)
    mixed, qgrad = call(place_q_kernel, [((TOK, LANES), BF)] * 2, (sel, router, att, dq),
                        cost=(4 * SLOTS * TOK * LANES, 3 << 20))
    pair, one = ((2 * SLOTS, 2 * HEAD_DIM), BF), ((SLOTS, 2 * HEAD_DIM), BF)
    up, down, across = call(add_far_kernel, [pair, pair, one], far, cost=(1 << 20, 2 << 20))
    across, up, down = along_z(across, 4), along_z(up, 2), along_z(down, 6)
    across, feat, mixed, qgrad = lax.optimization_barrier((across, feat, mixed, qgrad))
    own, nxt, prv = call(add_near_kernel, [one] * 3, (*near, up, down, across), cost=(1 << 20, 2 << 20))
    nxt, prv = along_z(nxt, 1), along_z(prv, 7)
    kgrad, vgrad, rgrad = call(
        place_kv_kernel,
        [((TOK, HEAD_DIM), BF)] * 2 + [((1, TOK), F32)],
        (sel, router, feat, own, nxt, prv),
        cost=(2 * SLOTS * TOK * 256, 1 << 20))
    return mixed, qgrad, kgrad, vgrad, rgrad.reshape(TOK)


def solution(mesh):
    inner = Mesh(mesh.devices.reshape(ROWS_Y, ROWS_Z, 8), ("y", "z", "mp"))
    seq = ("y", "z")
    in_specs = (P(seq, "mp"), P(seq, "mp"), P(seq, "mp"), P(seq, "mp"), P(seq), P(seq))
    out_specs = (P(seq, "mp"), P(seq, "mp"), P(seq, "mp"), P(seq, "mp"), P(seq))
    return jax.shard_map(shards, mesh=inner, in_specs=in_specs, out_specs=out_specs, check_vma=False)
```

```python
import functools

import jax
import jax.numpy as jnp
from jax import lax
from jax.experimental import pallas as pl
from jax.experimental.pallas import tpu as pltpu
from jax.sharding import Mesh, PartitionSpec as P

HEAD_DIM = 128
SLOTS = 128
TOK = 512
HEADS = 8
ROWS_Y = 4
ROWS_Z = 8
LANES = HEADS * HEAD_DIM
TILE = 512
GROUP = 16
SHARDS = ROWS_Y * ROWS_Z
PACKED = 2560
QCHUNK = 256
FAR = (2, 3, 6, 5, 4)
NEAR = (0, 1, 7)
FLAG = 64.0
NEG = -1e30
SCALE = HEAD_DIM ** (-0.5)
LOG2E = 1.4426950408889634
BF = jnp.bfloat16
F32 = jnp.float32
NT = (((1,), (1,)), ((), ()))
NN = (((1,), (0,)), ((), ()))
VMEM = pltpu.VMEM
LIMIT = 34 * 1024 * 1024


def dot(a, b, dims=NN):
    return lax.dot_general(a, b, dims, preferred_element_type=F32)


def column_of(row):
    return jnp.transpose(jnp.broadcast_to(row, (SLOTS, SLOTS)))


def picker(sel_row):
    col = column_of(sel_row.astype(F32))
    lane = lax.broadcasted_iota(jnp.int32, (SLOTS, SLOTS), 1).astype(F32)
    return jnp.concatenate([col == lane + float(c * SLOTS) for c in range(TOK // SLOTS)], axis=1)


def placer(sel_row):
    token = lax.broadcasted_iota(jnp.int32, (TOK, SLOTS), 0)
    return jnp.broadcast_to(sel_row, (TOK, SLOTS)) == token


def one_hot(mask):
    return jnp.where(mask, 1.0, 0.0).astype(BF)


def select_kv_kernel(sel_hbm, key_hbm, value_hbm, out_ref, sel_ref, key_ref, value_ref, sem):
    copies = [
        pltpu.make_async_copy(src, dst, sem.at[i])
        for i, (src, dst) in enumerate(((sel_hbm, sel_ref), (key_hbm, key_ref), (value_hbm, value_ref)))
    ]
    for c in copies:
        c.start()
    copies[0].wait()
    sel = sel_ref[...]
    pick = one_hot(picker(sel))
    live = column_of(sel.astype(F32)) >= 0.0
    copies[1].wait()
    key = jnp.where(live, dot(pick, key_ref[...]), FLAG).astype(BF)
    copies[2].wait()
    value = dot(pick, value_ref[...]).astype(BF)
    out_ref[:, :HEAD_DIM] = key
    out_ref[:, HEAD_DIM:] = value


def select_q_kernel(sel_ref, logit_ref, query_ref, cot_ref, q_ref, g_ref, c_ref, router_ref):
    mask = picker(sel_ref[...])
    pick = one_hot(mask)
    logit = jnp.sum(jnp.where(mask, logit_ref[...], 0.0), axis=1, keepdims=True)
    router = 1.0 / (1.0 + jnp.exp(-logit))
    router_ref[...] = jnp.broadcast_to(router, (SLOTS, SLOTS))
    for h in range(HEADS):
        cols = slice(h * HEAD_DIM, (h + 1) * HEAD_DIM)
        rows = slice(h * SLOTS, (h + 1) * SLOTS)
        q_ref[rows, :] = dot(pick, query_ref[:, cols]).astype(BF)
        cot = dot(pick, cot_ref[:, cols])
        c_ref[rows, :] = cot.astype(BF)
        g_ref[rows, :] = (router * cot).astype(BF)


def attention_kernel(pos_ref, ev0, ev1, ev2, ev3, od0, od1, od2, od3, q_ref, g_ref, c_ref,
                     att_hbm, dq_hbm, far0, far1, far2, far3, near0, near1, near2, near3, feat_ref,
                     kvs, dkv_ref, s_ref, w_ref, at_ref, dqt_ref, top_ref, sum_ref, cen_ref, tops_ref, att_ref, dq_ref, base_ref, sem):
    row = pos_ref[0]
    col = pos_ref[1]
    own = row * ROWS_Z + col
    at_ref[...] = jnp.zeros_like(at_ref)
    dqt_ref[...] = jnp.zeros_like(dqt_ref)
    top_ref[...] = jnp.full_like(top_ref, NEG)
    sum_ref[...] = jnp.zeros_like(sum_ref)

    evens, odds = (ev0, ev1, ev2, ev3), (od0, od1, od2, od3)

    def shard_rows(k, z):
        step = lax.rem(z - col + ROWS_Z, ROWS_Z)
        even = pl.multiple_of(lax.rem(step + 2, ROWS_Z) // 2 * SLOTS, SLOTS)
        odd = pl.multiple_of(step // 2 * SLOTS, SLOTS)
        return jnp.where(lax.rem(step, 2) == 0, evens[k][pl.ds(even, SLOTS), :], odds[k][pl.ds(odd, SLOTS), :])

    counts = {}
    for k in reversed(range(ROWS_Y)):
        for z in range(ROWS_Z):
            flags = shard_rows(k, z)[:, :HEAD_DIM].astype(F32) < 0.5 * FLAG
            live = jnp.sum(jnp.where(flags, 1.0, 0.0), axis=0, keepdims=True)
            count = jnp.max(live).astype(jnp.int32)
            past = z <= col if k == 0 else k <= row
            counts[k, z] = jnp.where(past, (count + (GROUP - 1)) // GROUP * GROUP, 0)
    base = jnp.int32(0)
    for k in reversed(range(ROWS_Y)):
        first = lax.rem(row - k + ROWS_Y, ROWS_Y) * ROWS_Z
        for z in range(ROWS_Z):
            base_ref[first + z] = base
            kvs[pl.ds(pl.multiple_of(base, GROUP), SLOTS), :] = shard_rows(k, z)
            base = base + counts[k, z]
    kvs[pl.ds(pl.multiple_of(base, GROUP), TILE), :] = jnp.zeros((TILE, 2 * HEAD_DIM), BF)
    query_id = base_ref[own]
    tiles = (base + (TILE - 1)) // TILE

    def scores(t, carry):
        rows = pl.ds(pl.multiple_of(t * TILE, TILE), TILE)
        keys = kvs[rows, :HEAD_DIM]
        kid = t * TILE + lax.broadcasted_iota(jnp.int32, (TILE, SLOTS), 0)
        qid = query_id + lax.broadcasted_iota(jnp.int32, (TILE, SLOTS), 1)
        dead = jnp.broadcast_to(keys[:, :1].astype(F32), (TILE, SLOTS)) > 0.5 * FLAG
        bias = jnp.where((kid > qid) | dead, NEG, 0.0)
        bias = jnp.concatenate([bias] * (QCHUNK // SLOTS), axis=1)
        for c in range(LANES // QCHUNK):
            lanes = slice(c * QCHUNK, (c + 1) * QCHUNK)
            s = dot(keys, q_ref[lanes, :], NT) * (SCALE * LOG2E) + bias
            s = s.reshape(TILE // 8, 8, QCHUNK)
            old = top_ref[:, lanes]
            new = jnp.maximum(old, jnp.max(s, axis=0))
            e = jnp.exp2(s - new[None])
            top_ref[:, lanes] = new
            tops_ref[t, :, lanes] = new
            sum_ref[:, lanes] = sum_ref[:, lanes] * jnp.exp2(old - new) + jnp.sum(e, axis=0)
            s_ref[rows, lanes] = e.reshape(TILE, QCHUNK)
        return carry

    lax.fori_loop(0, tiles, scores, 0)
    top = jnp.max(top_ref[...], axis=0, keepdims=True)
    total = jnp.sum(sum_ref[...] * jnp.exp2(top_ref[...] - top), axis=0, keepdims=True)
    top_ref[...] = jnp.broadcast_to(top, top_ref.shape)
    sum_ref[...] = jnp.broadcast_to(1.0 / total, sum_ref.shape)

    def forward(t, carry):
        rows = pl.ds(pl.multiple_of(t * TILE, TILE), TILE)
        values = kvs[rows, HEAD_DIM:]
        value_t = jnp.transpose(values)
        acc = jnp.zeros((TILE, HEAD_DIM), F32)
        for c in range(LANES // QCHUNK):
            lanes = slice(c * QCHUNK, (c + 1) * QCHUNK)
            factor = jnp.exp2(tops_ref[t, :, lanes] - top_ref[:, lanes]) * sum_ref[:, lanes]
            w = s_ref[rows, lanes].reshape(TILE // 8, 8, QCHUNK) * factor[None]
            w = w.reshape(TILE, QCHUNK).astype(BF)
            w_ref[rows, lanes] = w
            at_ref[:, lanes] += dot(value_t, w)
            acc += dot(w, g_ref[lanes, :])
            s_ref[rows, lanes] = dot(values, g_ref[lanes, :], NT)
        dkv_ref[rows, HEAD_DIM:] = acc.astype(BF)
        return carry

    lax.fori_loop(0, tiles, forward, 0)

    feature = jnp.zeros((SLOTS, HEAD_DIM), F32)
    for h in range(HEADS):
        lanes = slice(h * HEAD_DIM, (h + 1) * HEAD_DIM)
        att_t = at_ref[:, lanes].astype(BF)
        att = jnp.transpose(att_t)
        att_ref[:, lanes] = att
        grad_t = jnp.transpose(g_ref[lanes, :])
        centre = jnp.sum(grad_t.astype(F32) * att_t.astype(F32), axis=0, keepdims=True)
        cen_ref[:, lanes] = jnp.broadcast_to(centre, (8, HEAD_DIM))
        feature += c_ref[lanes, :].astype(F32) * att.astype(F32)
    feature = jnp.broadcast_to(jnp.sum(feature, axis=1, keepdims=True), (SLOTS, SLOTS))
    feature = jnp.transpose(feature)[:8, :]
    for peer in range(8):
        feat_ref[peer] = feature
    att_copy = pltpu.make_async_copy(att_ref, att_hbm, sem.at[0])
    att_copy.start()

    def backward(t, carry):
        rows = pl.ds(pl.multiple_of(t * TILE, TILE), TILE)
        key_t = jnp.transpose(kvs[rows, :HEAD_DIM])
        acc = jnp.zeros((TILE, HEAD_DIM), F32)
        for c in range(LANES // QCHUNK):
            lanes = slice(c * QCHUNK, (c + 1) * QCHUNK)
            slope = s_ref[rows, lanes].reshape(TILE // 8, 8, QCHUNK)
            w = w_ref[rows, lanes].astype(F32).reshape(TILE // 8, 8, QCHUNK)
            ds = (w * (slope - cen_ref[:, lanes][None]) * SCALE).reshape(TILE, QCHUNK).astype(BF)
            dqt_ref[:, lanes] += dot(key_t, ds)
            acc += dot(ds, q_ref[lanes, :])
        dkv_ref[rows, :HEAD_DIM] = acc.astype(BF)
        return carry

    lax.fori_loop(0, tiles, backward, 0)

    for h in range(HEADS):
        lanes = slice(h * HEAD_DIM, (h + 1) * HEAD_DIM)
        dq_ref[:, lanes] = jnp.transpose(dqt_ref[:, lanes].astype(BF))
    dq_copy = pltpu.make_async_copy(dq_ref, dq_hbm, sem.at[1])
    dq_copy.start()
    dkv_ref[pl.ds(pl.multiple_of(tiles * TILE, TILE), TILE), :] = jnp.zeros((TILE, 2 * HEAD_DIM), BF)
    for k, (far, near) in enumerate(((far0, near0), (far1, near1), (far2, near2), (far3, near3))):
        first = lax.rem(row + k, ROWS_Y) * ROWS_Z
        for out, steps in ((far, FAR), (near, NEAR)):
            for i, step in enumerate(steps):
                shard = first + lax.rem(col + step, ROWS_Z)
                rows = dkv_ref[pl.ds(pl.multiple_of(base_ref[shard], GROUP), SLOTS), :]
                out[i * SLOTS : (i + 1) * SLOTS, :] = jnp.where(shard <= own, rows, jnp.zeros_like(rows))
    att_copy.wait()
    dq_copy.wait()


def place_q_kernel(sel_ref, router_ref, att_ref, dq_ref, mixed_ref, qgrad_ref):
    place = one_hot(placer(sel_ref[...]))
    router = router_ref[...]
    for h in range(HEADS):
        lanes = slice(h * HEAD_DIM, (h + 1) * HEAD_DIM)
        mix = (router * att_ref[:, lanes].astype(F32)).astype(BF)
        mixed_ref[:, lanes] = dot(place, mix).astype(BF)
        qgrad_ref[:, lanes] = dot(place, dq_ref[:, lanes]).astype(BF)


def sum_of(*refs):
    total = refs[0][...].astype(F32)
    for ref in refs[1:]:
        total += ref[...].astype(F32)
    return total


def add_far_kernel(in0, in1, in2, in3, up_ref, down_ref, across_ref):
    total = sum_of(in0, in1, in2, in3).astype(BF)
    up_ref[...] = total[: 2 * SLOTS]
    down_ref[...] = total[2 * SLOTS : 4 * SLOTS]
    across_ref[...] = total[4 * SLOTS :]


def add_near_kernel(in0, in1, in2, in3, up_ref, down_ref, across_ref, own_ref, next_ref, prev_ref):
    total = sum_of(in0, in1, in2, in3)
    up = up_ref[...].astype(F32)
    down = down_ref[...].astype(F32)
    own_ref[...] = (total[:SLOTS] + up[:SLOTS] + down[:SLOTS] + across_ref[...].astype(F32)).astype(BF)
    next_ref[...] = (total[SLOTS : 2 * SLOTS] + up[SLOTS:]).astype(BF)
    prev_ref[...] = (total[2 * SLOTS :] + down[SLOTS:]).astype(BF)


def place_kv_kernel(sel_ref, router_ref, feat_ref, own_ref, prev_ref, next_ref, kgrad_ref, vgrad_ref, rgrad_ref):
    total = sum_of(own_ref, prev_ref, next_ref)
    placed = dot(one_hot(placer(sel_ref[...])), total.astype(BF)).astype(BF)
    kgrad_ref[...] = placed[:, :HEAD_DIM]
    vgrad_ref[...] = placed[:, HEAD_DIM:]
    feature = feat_ref[0]
    for k in range(1, 8):
        feature += feat_ref[k]
    router = router_ref[...]
    terms = router * (1.0 - router) * column_of(feature[:1, :])
    terms = jnp.concatenate([terms] * (TOK // SLOTS), axis=1)
    rgrad_ref[...] = jnp.sum(jnp.where(picker(sel_ref[...]), terms, 0.0), axis=0, keepdims=True)


def call(kernel, outs, args, scratch=(), specs=None, cost=None, limit=12 * 1024 * 1024, outside=0):
    return pl.pallas_call(
        kernel,
        out_shape=[jax.ShapeDtypeStruct(s, d) for s, d in outs],
        in_specs=specs or [pl.BlockSpec(memory_space=VMEM)] * len(args),
        out_specs=[pl.BlockSpec(memory_space=pltpu.HBM)] * outside + [pl.BlockSpec(memory_space=VMEM)] * (len(outs) - outside),
        scratch_shapes=list(scratch),
        compiler_params=pltpu.CompilerParams(vmem_limit_bytes=limit),
        cost_estimate=pl.CostEstimate(flops=cost[0], bytes_accessed=cost[1], transcendentals=0),
    )(*args)


def along_z(rows, step):
    return lax.ppermute(rows, "z", [(s, (s + step) % ROWS_Z) for s in range(ROWS_Z)])


def along_y(rows, step):
    return lax.ppermute(rows, "y", [(s, (s + step) % ROWS_Y) for s in range(ROWS_Y)])


def attend(pos, ev0, ev1, ev2, ev3, od0, od1, od2, od3, q, g, c):
    specs = [pl.BlockSpec(memory_space=pltpu.SMEM)] + [pl.BlockSpec(memory_space=VMEM)] * 11
    return call(
        attention_kernel,
        [((SLOTS, LANES), BF)] * 2 + [((len(FAR) * SLOTS, 2 * HEAD_DIM), BF)] * 4
        + [((len(NEAR) * SLOTS, 2 * HEAD_DIM), BF)] * 4 + [((8, 8, SLOTS), F32)],
        (pos, ev0, ev1, ev2, ev3, od0, od1, od2, od3, q, g, c),
        scratch=[
            VMEM((PACKED + TILE, 2 * HEAD_DIM), BF),
            VMEM((PACKED + TILE, 2 * HEAD_DIM), BF), VMEM((PACKED, LANES), F32), VMEM((PACKED, LANES), BF),
            VMEM((HEAD_DIM, LANES), F32), VMEM((HEAD_DIM, LANES), F32),
            VMEM((8, LANES), F32), VMEM((8, LANES), F32), VMEM((8, LANES), F32),
            VMEM((PACKED // TILE, 8, LANES), F32),
            VMEM((SLOTS, LANES), BF), VMEM((SLOTS, LANES), BF),
            pltpu.SMEM((SHARDS,), jnp.int32),
            pltpu.SemaphoreType.DMA((2,)),
        ],
        specs=specs,
        cost=(12 * PACKED * LANES * HEAD_DIM, 8 << 20),
        limit=LIMIT, outside=2)


def shards(query_rows, key_rows, value_rows, cotangent, router_logits, selection):
    sel = selection.reshape(1, SLOTS)
    logits = router_logits.reshape(1, TOK)
    row = lax.axis_index("y")
    col = lax.axis_index("z")
    (own,) = call(select_kv_kernel, [((SLOTS, 2 * HEAD_DIM), BF)], (sel, key_rows, value_rows),
                  scratch=[VMEM((1, SLOTS), jnp.int32), VMEM((TOK, HEAD_DIM), BF), VMEM((TOK, HEAD_DIM), BF),
                           pltpu.SemaphoreType.DMA((3,))],
                  specs=[pl.BlockSpec(memory_space=pltpu.HBM)] * 3,
                  cost=(2 * SLOTS * TOK * 256, 1 << 20), limit=60 * 1024 * 1024)
    across, up, down = along_z(own, 4), along_z(own, 2), along_z(own, 6)
    even = jnp.concatenate([up, own, down, across], axis=0)
    near, far = along_z(even[SLOTS : 3 * SLOTS], 7), along_z(even[: 2 * SLOTS], 1)
    evens = [even] + [along_y(even, k) for k in range(1, ROWS_Y)]
    odd = jnp.concatenate([near, far], axis=0)
    odds = [odd] + [along_y(odd, k) for k in range(1, ROWS_Y)]
    q, g, c, router = call(
        select_q_kernel,
        [((LANES, HEAD_DIM), BF)] * 3 + [((SLOTS, SLOTS), F32)],
        (sel, logits, query_rows, cotangent),
        cost=(4 * SLOTS * TOK * LANES, 3 << 20))
    pos = jnp.stack([row, col]).astype(jnp.int32)
    att, dq, *parts, feat = attend(pos, *evens, *odds, q, g, c)
    far = [parts[0]] + [along_y(parts[k], k) for k in range(1, ROWS_Y)]
    near = [parts[4]] + [along_y(parts[4 + k], k) for k in range(1, ROWS_Y)]
    feat = lax.all_to_all(feat, "mp", 0, 0, tiled=True)
    mixed, qgrad = call(place_q_kernel, [((TOK, LANES), BF)] * 2, (sel, router, att, dq),
                        cost=(4 * SLOTS * TOK * LANES, 3 << 20))
    far[3], feat = lax.optimization_barrier((far[3], feat))
    pair, one = ((2 * SLOTS, 2 * HEAD_DIM), BF), ((SLOTS, 2 * HEAD_DIM), BF)
    up, down, across = call(add_far_kernel, [pair, pair, one], far, cost=(1 << 20, 2 << 20))
    across, up, down = along_z(across, 4), along_z(up, 2), along_z(down, 6)
    across, mixed, qgrad = lax.optimization_barrier((across, mixed, qgrad))
    own, nxt, prv = call(add_near_kernel, [one] * 3, (*near, up, down, across), cost=(1 << 20, 2 << 20))
    nxt, prv = along_z(nxt, 1), along_z(prv, 7)
    kgrad, vgrad, rgrad = call(
        place_kv_kernel,
        [((TOK, HEAD_DIM), BF)] * 2 + [((1, TOK), F32)],
        (sel, router, feat, own, nxt, prv),
        cost=(2 * SLOTS * TOK * 256, 1 << 20))
    return mixed, qgrad, kgrad, vgrad, rgrad.reshape(TOK)


def solution(mesh):
    inner = Mesh(mesh.devices.reshape(ROWS_Y, ROWS_Z, 8), ("y", "z", "mp"))
    seq = ("y", "z")
    in_specs = (P(seq, "mp"), P(seq, "mp"), P(seq, "mp"), P(seq, "mp"), P(seq), P(seq))
    out_specs = (P(seq, "mp"), P(seq, "mp"), P(seq, "mp"), P(seq, "mp"), P(seq))
    return jax.shard_map(shards, mesh=inner, in_specs=in_specs, out_specs=out_specs, check_vma=False)
```

```python
import jax
import jax.numpy as jnp
from jax import lax
from jax.experimental import pallas as pl
from jax.experimental.pallas import tpu as pltpu
from jax.sharding import Mesh, PartitionSpec as P

HEAD_DIM = 128
SLOTS = 128
TOK = 512
HEADS = 8
ROWS_Y = 4
ROWS_Z = 8
LANES = HEADS * HEAD_DIM
TILE = 512
GROUP = 16
SHARDS = ROWS_Y * ROWS_Z
PACKED = 2560
QCHUNK = 256
FAR = (2, 3, 6, 5, 4)
NEAR = (0, 1, 7)
FLAG = 64.0
NEG = -1e30
SCALE = HEAD_DIM ** (-0.5)
LOG2E = 1.4426950408889634
BF = jnp.bfloat16
F32 = jnp.float32
NT = (((1,), (1,)), ((), ()))
NN = (((1,), (0,)), ((), ()))
VMEM = pltpu.VMEM
LIMIT = 34 * 1024 * 1024


def dot(a, b, dims=NN):
    return lax.dot_general(a, b, dims, preferred_element_type=F32)


def column_of(row):
    return jnp.transpose(jnp.broadcast_to(row, (SLOTS, SLOTS)))


def picker(sel_row):
    col = column_of(sel_row.astype(F32))
    lane = lax.broadcasted_iota(jnp.int32, (SLOTS, SLOTS), 1).astype(F32)
    return jnp.concatenate([col == lane + float(c * SLOTS) for c in range(TOK // SLOTS)], axis=1)


def placer(sel_row):
    token = lax.broadcasted_iota(jnp.int32, (TOK, SLOTS), 0)
    return jnp.broadcast_to(sel_row, (TOK, SLOTS)) == token


def one_hot(mask):
    return jnp.where(mask, 1.0, 0.0).astype(BF)


def select_kv_kernel(sel_hbm, key_hbm, value_hbm, out_ref, sel_ref, key_ref, value_ref, sem):
    copies = [
        pltpu.make_async_copy(src, dst, sem.at[i])
        for i, (src, dst) in enumerate(((sel_hbm, sel_ref), (key_hbm, key_ref), (value_hbm, value_ref)))
    ]
    for c in copies:
        c.start()
    copies[0].wait()
    sel = sel_ref[...]
    pick = one_hot(picker(sel))
    live = column_of(sel.astype(F32)) >= 0.0
    copies[1].wait()
    key = jnp.where(live, dot(pick, key_ref[...]), FLAG).astype(BF)
    copies[2].wait()
    value = dot(pick, value_ref[...]).astype(BF)
    out_ref[:, :HEAD_DIM] = key
    out_ref[:, HEAD_DIM:] = value


def select_q_kernel(sel_ref, logit_ref, query_ref, cot_ref, q_ref, g_ref, c_ref, router_ref):
    mask = picker(sel_ref[...])
    pick = one_hot(mask)
    logit = jnp.sum(jnp.where(mask, logit_ref[...], 0.0), axis=1, keepdims=True)
    router = 1.0 / (1.0 + jnp.exp(-logit))
    router_ref[...] = jnp.broadcast_to(router, (SLOTS, SLOTS))
    for h in range(HEADS):
        cols = slice(h * HEAD_DIM, (h + 1) * HEAD_DIM)
        rows = slice(h * SLOTS, (h + 1) * SLOTS)
        q_ref[rows, :] = dot(pick, query_ref[:, cols]).astype(BF)
        cot = dot(pick, cot_ref[:, cols])
        c_ref[rows, :] = cot.astype(BF)
        g_ref[rows, :] = (router * cot).astype(BF)


def attention_kernel(pos_ref, ev0, ev1, ev2, ev3, od0, od1, od2, od3, q_ref, g_ref, c_ref,
                     att_hbm, dq_hbm, far0, far1, far2, far3, near0, near1, near2, near3, feat_ref,
                     kvs, dkv_ref, s_ref, w_ref, at_ref, dqt_ref, top_ref, sum_ref, cen_ref, tops_ref, att_ref, dq_ref, base_ref, sem):
    row = pos_ref[0]
    col = pos_ref[1]
    own = row * ROWS_Z + col
    at_ref[...] = jnp.zeros_like(at_ref)
    dqt_ref[...] = jnp.zeros_like(dqt_ref)
    top_ref[...] = jnp.full_like(top_ref, NEG)
    sum_ref[...] = jnp.zeros_like(sum_ref)

    evens, odds = (ev0, ev1, ev2, ev3), (od0, od1, od2, od3)

    def shard_rows(k, z):
        step = lax.rem(z - col + ROWS_Z, ROWS_Z)
        first = (lax.rem(step, 2) == 0) & (step != 4)
        early = jnp.where(first, lax.rem(step + 2, ROWS_Z) // 2, 0)
        late = jnp.where(step == 4, 4, step // 2)
        early = evens[k][pl.ds(pl.multiple_of(early * SLOTS, SLOTS), SLOTS), :]
        late = odds[k][pl.ds(pl.multiple_of(late * SLOTS, SLOTS), SLOTS), :]
        return jnp.where(first, early, late)

    counts = {}
    for k in reversed(range(ROWS_Y)):
        for z in range(ROWS_Z):
            flags = shard_rows(k, z)[:, :HEAD_DIM].astype(F32) < 0.5 * FLAG
            live = jnp.sum(jnp.where(flags, 1.0, 0.0), axis=0, keepdims=True)
            count = jnp.max(live).astype(jnp.int32)
            past = z <= col if k == 0 else k <= row
            counts[k, z] = jnp.where(past, (count + (GROUP - 1)) // GROUP * GROUP, 0)
    base = jnp.int32(0)
    for k in reversed(range(ROWS_Y)):
        first = lax.rem(row - k + ROWS_Y, ROWS_Y) * ROWS_Z
        for z in range(ROWS_Z):
            base_ref[first + z] = base
            kvs[pl.ds(pl.multiple_of(base, GROUP), SLOTS), :] = shard_rows(k, z)
            base = base + counts[k, z]
    kvs[pl.ds(pl.multiple_of(base, GROUP), TILE), :] = jnp.zeros((TILE, 2 * HEAD_DIM), BF)
    query_id = base_ref[own]
    tiles = (base + (TILE - 1)) // TILE

    def scores(t, carry):
        rows = pl.ds(pl.multiple_of(t * TILE, TILE), TILE)
        keys = kvs[rows, :HEAD_DIM]
        kid = t * TILE + lax.broadcasted_iota(jnp.int32, (TILE, SLOTS), 0)
        qid = query_id + lax.broadcasted_iota(jnp.int32, (TILE, SLOTS), 1)
        dead = jnp.broadcast_to(keys[:, :1].astype(F32), (TILE, SLOTS)) > 0.5 * FLAG
        bias = jnp.where((kid > qid) | dead, NEG, 0.0)
        bias = jnp.concatenate([bias] * (QCHUNK // SLOTS), axis=1)
        for c in range(LANES // QCHUNK):
            lanes = slice(c * QCHUNK, (c + 1) * QCHUNK)
            s = dot(keys, q_ref[lanes, :], NT) * (SCALE * LOG2E) + bias
            s = s.reshape(TILE // 8, 8, QCHUNK)
            old = top_ref[:, lanes]
            new = jnp.maximum(old, jnp.max(s, axis=0))
            e = jnp.exp2(s - new[None])
            top_ref[:, lanes] = new
            tops_ref[t, :, lanes] = new
            sum_ref[:, lanes] = sum_ref[:, lanes] * jnp.exp2(old - new) + jnp.sum(e, axis=0)
            s_ref[rows, lanes] = e.reshape(TILE, QCHUNK)
        return carry

    lax.fori_loop(0, tiles, scores, 0)
    top = jnp.max(top_ref[...], axis=0, keepdims=True)
    total = jnp.sum(sum_ref[...] * jnp.exp2(top_ref[...] - top), axis=0, keepdims=True)
    top_ref[...] = jnp.broadcast_to(top, top_ref.shape)
    sum_ref[...] = jnp.broadcast_to(1.0 / total, sum_ref.shape)

    def forward(t, carry):
        rows = pl.ds(pl.multiple_of(t * TILE, TILE), TILE)
        values = kvs[rows, HEAD_DIM:]
        value_t = jnp.transpose(values)
        acc = jnp.zeros((TILE, HEAD_DIM), F32)
        for c in range(LANES // QCHUNK):
            lanes = slice(c * QCHUNK, (c + 1) * QCHUNK)
            factor = jnp.exp2(tops_ref[t, :, lanes] - top_ref[:, lanes]) * sum_ref[:, lanes]
            w = s_ref[rows, lanes].reshape(TILE // 8, 8, QCHUNK) * factor[None]
            w = w.reshape(TILE, QCHUNK).astype(BF)
            w_ref[rows, lanes] = w
            at_ref[:, lanes] += dot(value_t, w)
            acc += dot(w, g_ref[lanes, :])
            s_ref[rows, lanes] = dot(values, g_ref[lanes, :], NT)
        dkv_ref[rows, HEAD_DIM:] = acc.astype(BF)
        return carry

    lax.fori_loop(0, tiles, forward, 0)

    feature = jnp.zeros((SLOTS, HEAD_DIM), F32)
    for h in range(HEADS):
        lanes = slice(h * HEAD_DIM, (h + 1) * HEAD_DIM)
        att_t = at_ref[:, lanes].astype(BF)
        att = jnp.transpose(att_t)
        att_ref[:, lanes] = att
        grad_t = jnp.transpose(g_ref[lanes, :])
        centre = jnp.sum(grad_t.astype(F32) * att_t.astype(F32), axis=0, keepdims=True)
        cen_ref[:, lanes] = jnp.broadcast_to(centre, (8, HEAD_DIM))
        feature += c_ref[lanes, :].astype(F32) * att.astype(F32)
    feature = jnp.broadcast_to(jnp.sum(feature, axis=1, keepdims=True), (SLOTS, SLOTS))
    feature = jnp.transpose(feature)[:8, :]
    for peer in range(8):
        feat_ref[peer] = feature
    att_copy = pltpu.make_async_copy(att_ref, att_hbm, sem.at[0])
    att_copy.start()

    def backward(t, carry):
        rows = pl.ds(pl.multiple_of(t * TILE, TILE), TILE)
        key_t = jnp.transpose(kvs[rows, :HEAD_DIM])
        acc = jnp.zeros((TILE, HEAD_DIM), F32)
        for c in range(LANES // QCHUNK):
            lanes = slice(c * QCHUNK, (c + 1) * QCHUNK)
            slope = s_ref[rows, lanes].reshape(TILE // 8, 8, QCHUNK)
            w = w_ref[rows, lanes].astype(F32).reshape(TILE // 8, 8, QCHUNK)
            ds = (w * (slope - cen_ref[:, lanes][None]) * SCALE).reshape(TILE, QCHUNK).astype(BF)
            w_ref[rows, lanes] = ds
            acc += dot(ds, q_ref[lanes, :])
        dkv_ref[rows, :HEAD_DIM] = acc.astype(BF)
        dqt_ref[...] += dot(key_t, w_ref[rows, :])
        return carry

    lax.fori_loop(0, tiles, backward, 0)

    for h in range(HEADS):
        lanes = slice(h * HEAD_DIM, (h + 1) * HEAD_DIM)
        dq_ref[:, lanes] = jnp.transpose(dqt_ref[:, lanes].astype(BF))
    dq_copy = pltpu.make_async_copy(dq_ref, dq_hbm, sem.at[1])
    dq_copy.start()
    dkv_ref[pl.ds(pl.multiple_of(tiles * TILE, TILE), TILE), :] = jnp.zeros((TILE, 2 * HEAD_DIM), BF)
    for k, (far, near) in enumerate(((far0, near0), (far1, near1), (far2, near2), (far3, near3))):
        first = lax.rem(row + k, ROWS_Y) * ROWS_Z
        for out, steps in ((far, FAR), (near, NEAR)):
            for i, step in enumerate(steps):
                shard = first + lax.rem(col + step, ROWS_Z)
                rows = dkv_ref[pl.ds(pl.multiple_of(base_ref[shard], GROUP), SLOTS), :]
                out[i * SLOTS : (i + 1) * SLOTS, :] = jnp.where(shard <= own, rows, jnp.zeros_like(rows))
    att_copy.wait()
    dq_copy.wait()


def place_q_kernel(sel_ref, router_ref, att_ref, dq_ref, mixed_ref, qgrad_ref):
    place = one_hot(placer(sel_ref[...]))
    router = router_ref[...]
    for h in range(HEADS):
        lanes = slice(h * HEAD_DIM, (h + 1) * HEAD_DIM)
        mix = (router * att_ref[:, lanes].astype(F32)).astype(BF)
        mixed_ref[:, lanes] = dot(place, mix).astype(BF)
        qgrad_ref[:, lanes] = dot(place, dq_ref[:, lanes]).astype(BF)


def sum_of(*refs):
    total = refs[0][...].astype(F32)
    for ref in refs[1:]:
        total += ref[...].astype(F32)
    return total


def add_far_kernel(in0, in1, in2, in3, up_ref, down_ref, across_ref):
    total = sum_of(in0, in1, in2, in3).astype(BF)
    up_ref[...] = total[: 2 * SLOTS]
    down_ref[...] = total[2 * SLOTS : 4 * SLOTS]
    across_ref[...] = total[4 * SLOTS :]


def add_near_kernel(in0, in1, in2, in3, up_ref, down_ref, across_ref, own_ref, next_ref, prev_ref):
    total = sum_of(in0, in1, in2, in3)
    up = up_ref[...].astype(F32)
    down = down_ref[...].astype(F32)
    own_ref[...] = (total[:SLOTS] + up[:SLOTS] + down[:SLOTS] + across_ref[...].astype(F32)).astype(BF)
    next_ref[...] = (total[SLOTS : 2 * SLOTS] + up[SLOTS:]).astype(BF)
    prev_ref[...] = (total[2 * SLOTS :] + down[SLOTS:]).astype(BF)


def place_kv_kernel(sel_ref, router_ref, feat_ref, own_ref, prev_ref, next_ref, kgrad_ref, vgrad_ref, rgrad_ref):
    total = sum_of(own_ref, prev_ref, next_ref)
    placed = dot(one_hot(placer(sel_ref[...])), total.astype(BF)).astype(BF)
    kgrad_ref[...] = placed[:, :HEAD_DIM]
    vgrad_ref[...] = placed[:, HEAD_DIM:]
    feature = feat_ref[0]
    for k in range(1, 8):
        feature += feat_ref[k]
    router = router_ref[...]
    terms = router * (1.0 - router) * column_of(feature[:1, :])
    terms = jnp.concatenate([terms] * (TOK // SLOTS), axis=1)
    rgrad_ref[...] = jnp.sum(jnp.where(picker(sel_ref[...]), terms, 0.0), axis=0, keepdims=True)


def call(kernel, outs, args, scratch=(), specs=None, cost=None, limit=12 * 1024 * 1024, outside=0):
    return pl.pallas_call(
        kernel,
        out_shape=[jax.ShapeDtypeStruct(s, d) for s, d in outs],
        in_specs=specs or [pl.BlockSpec(memory_space=VMEM)] * len(args),
        out_specs=[pl.BlockSpec(memory_space=pltpu.HBM)] * outside + [pl.BlockSpec(memory_space=VMEM)] * (len(outs) - outside),
        scratch_shapes=list(scratch),
        compiler_params=pltpu.CompilerParams(vmem_limit_bytes=limit),
        cost_estimate=pl.CostEstimate(flops=cost[0], bytes_accessed=cost[1], transcendentals=0),
    )(*args)


def along_z(rows, step):
    return lax.ppermute(rows, "z", [(s, (s + step) % ROWS_Z) for s in range(ROWS_Z)])


def along_y(rows, step):
    return lax.ppermute(rows, "y", [(s, (s + step) % ROWS_Y) for s in range(ROWS_Y)])


def attend(pos, ev0, ev1, ev2, ev3, od0, od1, od2, od3, q, g, c):
    specs = [pl.BlockSpec(memory_space=pltpu.SMEM)] + [pl.BlockSpec(memory_space=VMEM)] * 11
    return call(
        attention_kernel,
        [((SLOTS, LANES), BF)] * 2 + [((len(FAR) * SLOTS, 2 * HEAD_DIM), BF)] * 4
        + [((len(NEAR) * SLOTS, 2 * HEAD_DIM), BF)] * 4 + [((8, 8, SLOTS), F32)],
        (pos, ev0, ev1, ev2, ev3, od0, od1, od2, od3, q, g, c),
        scratch=[
            VMEM((PACKED + TILE, 2 * HEAD_DIM), BF),
            VMEM((PACKED + TILE, 2 * HEAD_DIM), BF), VMEM((PACKED, LANES), F32), VMEM((PACKED, LANES), BF),
            VMEM((HEAD_DIM, LANES), F32), VMEM((HEAD_DIM, LANES), F32),
            VMEM((8, LANES), F32), VMEM((8, LANES), F32), VMEM((8, LANES), F32),
            VMEM((PACKED // TILE, 8, LANES), F32),
            VMEM((SLOTS, LANES), BF), VMEM((SLOTS, LANES), BF),
            pltpu.SMEM((SHARDS,), jnp.int32),
            pltpu.SemaphoreType.DMA((2,)),
        ],
        specs=specs,
        cost=(12 * PACKED * LANES * HEAD_DIM, 8 << 20),
        limit=LIMIT, outside=2)


def shards(query_rows, key_rows, value_rows, cotangent, router_logits, selection):
    sel = selection.reshape(1, SLOTS)
    logits = router_logits.reshape(1, TOK)
    row = lax.axis_index("y")
    col = lax.axis_index("z")
    (own,) = call(select_kv_kernel, [((SLOTS, 2 * HEAD_DIM), BF)], (sel, key_rows, value_rows),
                  scratch=[VMEM((1, SLOTS), jnp.int32), VMEM((TOK, HEAD_DIM), BF), VMEM((TOK, HEAD_DIM), BF),
                           pltpu.SemaphoreType.DMA((3,))],
                  specs=[pl.BlockSpec(memory_space=pltpu.HBM)] * 3,
                  cost=(2 * SLOTS * TOK * 256, 1 << 20), limit=60 * 1024 * 1024)
    across, up, down = along_z(own, 4), along_z(own, 2), along_z(own, 6)
    even = jnp.concatenate([up, own, down], axis=0)
    near, far = along_z(even[SLOTS : 3 * SLOTS], 7), along_z(even[: 2 * SLOTS], 1)
    evens = [even]
    for k in range(1, ROWS_Y):
        evens.append(along_y(even, k))
    odd = jnp.concatenate([near, far, across], axis=0)
    odds = [odd]
    for k in range(1, ROWS_Y):
        odds.append(along_y(odd, k))
    q, g, c, router = call(
        select_q_kernel,
        [((LANES, HEAD_DIM), BF)] * 3 + [((SLOTS, SLOTS), F32)],
        (sel, logits, query_rows, cotangent),
        cost=(4 * SLOTS * TOK * LANES, 3 << 20))
    pos = jnp.stack([row, col]).astype(jnp.int32)
    att, dq, *parts, feat = attend(pos, *evens, *odds, q, g, c)
    far = [parts[0]] + [along_y(parts[k], k) for k in range(1, ROWS_Y)]
    near = [parts[4]] + [along_y(parts[4 + k], k) for k in range(1, ROWS_Y)]
    feat = lax.all_to_all(feat, "mp", 0, 0, tiled=True)
    mixed, qgrad = call(place_q_kernel, [((TOK, LANES), BF)] * 2, (sel, router, att, dq),
                        cost=(4 * SLOTS * TOK * LANES, 3 << 20))
    far[3], feat = lax.optimization_barrier((far[3], feat))
    pair, one = ((2 * SLOTS, 2 * HEAD_DIM), BF), ((SLOTS, 2 * HEAD_DIM), BF)
    up, down, across = call(add_far_kernel, [pair, pair, one], far, cost=(1 << 20, 2 << 20))
    across = along_z(across, 4)
    up = along_z(up, 2)
    down = along_z(down, 6)
    across, mixed, qgrad = lax.optimization_barrier((across, mixed, qgrad))
    own, nxt, prv = call(add_near_kernel, [one] * 3, (*near, up, down, across), cost=(1 << 20, 2 << 20))
    nxt, prv = along_z(nxt, 1), along_z(prv, 7)
    kgrad, vgrad, rgrad = call(
        place_kv_kernel,
        [((TOK, HEAD_DIM), BF)] * 2 + [((1, TOK), F32)],
        (sel, router, feat, own, nxt, prv),
        cost=(2 * SLOTS * TOK * 256, 1 << 20))
    return mixed, qgrad, kgrad, vgrad, rgrad.reshape(TOK)


def solution(mesh):
    inner = Mesh(mesh.devices.reshape(ROWS_Y, ROWS_Z, 8), ("y", "z", "mp"))
    seq = ("y", "z")
    in_specs = (P(seq, "mp"), P(seq, "mp"), P(seq, "mp"), P(seq, "mp"), P(seq), P(seq))
    out_specs = (P(seq, "mp"), P(seq, "mp"), P(seq, "mp"), P(seq, "mp"), P(seq))

    return jax.shard_map(shards, mesh=inner, in_specs=in_specs, out_specs=out_specs, check_vma=False)
```

```python
import jax
import jax.numpy as jnp
from jax import lax
from jax.experimental import pallas as pl
from jax.experimental.pallas import tpu as pltpu
from jax.sharding import Mesh, PartitionSpec as P

HEAD_DIM = 128
SLOTS = 128
TOK = 512
HEADS = 8
ROWS_Y = 4
ROWS_Z = 8
LANES = HEADS * HEAD_DIM
TILE = 512
GROUP = 16
SHARDS = ROWS_Y * ROWS_Z
PACKED = 2560
QCHUNK = 256
FAR = (2, 3, 6, 5, 4)
NEAR = (0, 1, 7)
FLAG = 64.0
NEG = -1e30
SCALE = HEAD_DIM ** (-0.5)
LOG2E = 1.4426950408889634
BF = jnp.bfloat16
F32 = jnp.float32
NT = (((1,), (1,)), ((), ()))
NN = (((1,), (0,)), ((), ()))
VMEM = pltpu.VMEM
LIMIT = 46 * 1024 * 1024


def dot(a, b, dims=NN):
    return lax.dot_general(a, b, dims, preferred_element_type=F32)


def column_of(row):
    return jnp.transpose(jnp.broadcast_to(row, (SLOTS, SLOTS)))


def picker(sel_row):
    col = column_of(sel_row.astype(F32))
    lane = lax.broadcasted_iota(jnp.int32, (SLOTS, SLOTS), 1).astype(F32)
    return jnp.concatenate([col == lane + float(c * SLOTS) for c in range(TOK // SLOTS)], axis=1)


def placer(sel_row):
    token = lax.broadcasted_iota(jnp.int32, (TOK, SLOTS), 0)
    return jnp.broadcast_to(sel_row, (TOK, SLOTS)) == token


def one_hot(mask):
    return jnp.where(mask, 1.0, 0.0).astype(BF)


def select_kv_kernel(sel_hbm, key_hbm, value_hbm, out_ref, sel_ref, key_ref, value_ref, sem):
    copies = [
        pltpu.make_async_copy(src, dst, sem.at[i])
        for i, (src, dst) in enumerate(((sel_hbm, sel_ref), (key_hbm, key_ref), (value_hbm, value_ref)))
    ]
    for c in copies:
        c.start()
    copies[0].wait()
    sel = sel_ref[...]
    pick = one_hot(picker(sel))
    live = column_of(sel.astype(F32)) >= 0.0
    copies[1].wait()
    key = jnp.where(live, dot(pick, key_ref[...]), FLAG).astype(BF)
    copies[2].wait()
    value = dot(pick, value_ref[...]).astype(BF)
    out_ref[:, :HEAD_DIM] = key
    out_ref[:, HEAD_DIM:] = value


def select_q_kernel(sel_ref, logit_ref, query_ref, cot_ref, q_ref, g_ref, c_ref, router_ref):
    mask = picker(sel_ref[...])
    pick = one_hot(mask)
    logit = jnp.sum(jnp.where(mask, logit_ref[...], 0.0), axis=1, keepdims=True)
    router = 1.0 / (1.0 + jnp.exp(-logit))
    router_ref[...] = jnp.broadcast_to(router, (SLOTS, SLOTS))
    for h in range(HEADS):
        cols = slice(h * HEAD_DIM, (h + 1) * HEAD_DIM)
        rows = slice(h * SLOTS, (h + 1) * SLOTS)
        q_ref[rows, :] = dot(pick, query_ref[:, cols]).astype(BF)
        cot = dot(pick, cot_ref[:, cols])
        c_ref[rows, :] = cot.astype(BF)
        g_ref[rows, :] = (router * cot).astype(BF)


def attention_kernel(pos_ref, ow0, ow1, ow2, ow3, ev0, ev1, ev2, ev3, od0, od1, od2, od3, q_ref, g_ref, c_ref,
                     att_hbm, dq_hbm, far0, far1, far2, far3, near0, near1, near2, near3, feat_ref,
                     kvs, dkv_ref, s_ref, d_ref, w_ref, at_ref, dqt_ref, top_ref, sum_ref, cen_ref, tops_ref, att_ref, dq_ref, base_ref, sem):
    row = pos_ref[0]
    col = pos_ref[1]
    own = row * ROWS_Z + col
    at_ref[...] = jnp.zeros_like(at_ref)
    dqt_ref[...] = jnp.zeros_like(dqt_ref)
    top_ref[...] = jnp.full_like(top_ref, NEG)
    sum_ref[...] = jnp.zeros_like(sum_ref)

    owns, evens, odds = (ow0, ow1, ow2, ow3), (ev0, ev1, ev2, ev3), (od0, od1, od2, od3)

    def shard_rows(k, z):
        step = lax.rem(z - col + ROWS_Z, ROWS_Z)
        half = step // 2
        even = evens[k][pl.ds(pl.multiple_of(jnp.maximum(half - 1, 0) * SLOTS, SLOTS), SLOTS), :]
        odd = odds[k][pl.ds(pl.multiple_of(half * SLOTS, SLOTS), SLOTS), :]
        return jnp.where(step == 0, owns[k][...], jnp.where(lax.rem(step, 2) == 0, even, odd))

    counts = {}
    for k in reversed(range(ROWS_Y)):
        for z in range(ROWS_Z):
            flags = shard_rows(k, z)[:, :HEAD_DIM].astype(F32) < 0.5 * FLAG
            live = jnp.sum(jnp.where(flags, 1.0, 0.0), axis=0, keepdims=True)
            count = jnp.max(live).astype(jnp.int32)
            past = z <= col if k == 0 else k <= row
            counts[k, z] = jnp.where(past, (count + (GROUP - 1)) // GROUP * GROUP, 0)
    base = jnp.int32(0)
    for k in reversed(range(ROWS_Y)):
        first = lax.rem(row - k + ROWS_Y, ROWS_Y) * ROWS_Z
        for z in range(ROWS_Z):
            base_ref[first + z] = base
            kvs[pl.ds(pl.multiple_of(base, GROUP), SLOTS), :] = shard_rows(k, z)
            base = base + counts[k, z]
    kvs[pl.ds(pl.multiple_of(base, GROUP), TILE), :] = jnp.zeros((TILE, 2 * HEAD_DIM), BF)
    query_id = base_ref[own]
    tiles = (base + (TILE - 1)) // TILE

    def scores(t, carry):
        rows = pl.ds(pl.multiple_of(t * TILE, TILE), TILE)
        keys = kvs[rows, :HEAD_DIM]
        kid = t * TILE + lax.broadcasted_iota(jnp.int32, (TILE, SLOTS), 0)
        qid = query_id + lax.broadcasted_iota(jnp.int32, (TILE, SLOTS), 1)
        dead = jnp.broadcast_to(keys[:, :1].astype(F32), (TILE, SLOTS)) > 0.5 * FLAG
        bias = jnp.where((kid > qid) | dead, NEG, 0.0)
        bias = jnp.concatenate([bias] * (QCHUNK // SLOTS), axis=1)
        for c in range(LANES // QCHUNK):
            lanes = slice(c * QCHUNK, (c + 1) * QCHUNK)
            s = dot(keys, q_ref[lanes, :], NT) * (SCALE * LOG2E) + bias
            s = s.reshape(TILE // 8, 8, QCHUNK)
            old = top_ref[:, lanes]
            new = jnp.maximum(old, jnp.max(s, axis=0))
            e = jnp.exp2(s - new[None])
            top_ref[:, lanes] = new
            tops_ref[t, :, lanes] = new
            sum_ref[:, lanes] = sum_ref[:, lanes] * jnp.exp2(old - new) + jnp.sum(e, axis=0)
            s_ref[rows, lanes] = e.reshape(TILE, QCHUNK)
            d_ref[rows, lanes] = dot(kvs[rows, HEAD_DIM:], g_ref[lanes, :], NT)
        return carry

    lax.fori_loop(0, tiles, scores, 0)
    top = jnp.max(top_ref[...], axis=0, keepdims=True)
    total = jnp.sum(sum_ref[...] * jnp.exp2(top_ref[...] - top), axis=0, keepdims=True)
    top_ref[...] = jnp.broadcast_to(top, top_ref.shape)
    sum_ref[...] = jnp.broadcast_to(1.0 / total, sum_ref.shape)

    def forward(t, carry):
        rows = pl.ds(pl.multiple_of(t * TILE, TILE), TILE)
        values = kvs[rows, HEAD_DIM:]
        value_t = jnp.transpose(values)
        acc = jnp.zeros((TILE, HEAD_DIM), F32)
        for c in range(LANES // QCHUNK):
            lanes = slice(c * QCHUNK, (c + 1) * QCHUNK)
            factor = jnp.exp2(tops_ref[t, :, lanes] - top_ref[:, lanes]) * sum_ref[:, lanes]
            w = s_ref[rows, lanes].reshape(TILE // 8, 8, QCHUNK) * factor[None]
            w = w.reshape(TILE, QCHUNK).astype(BF)
            w_ref[rows, lanes] = w
            acc += dot(w, g_ref[lanes, :])
        dkv_ref[rows, HEAD_DIM:] = acc.astype(BF)
        at_ref[...] += dot(value_t, w_ref[rows, :])
        return carry

    lax.fori_loop(0, tiles, forward, 0)

    feature = jnp.zeros((SLOTS, HEAD_DIM), F32)
    for h in range(HEADS):
        lanes = slice(h * HEAD_DIM, (h + 1) * HEAD_DIM)
        att_t = at_ref[:, lanes].astype(BF)
        att = jnp.transpose(att_t)
        att_ref[:, lanes] = att
        grad_t = jnp.transpose(g_ref[lanes, :])
        centre = jnp.sum(grad_t.astype(F32) * att_t.astype(F32), axis=0, keepdims=True)
        cen_ref[:, lanes] = jnp.broadcast_to(centre, (8, HEAD_DIM))
        feature += c_ref[lanes, :].astype(F32) * att.astype(F32)
    feature = jnp.broadcast_to(jnp.sum(feature, axis=1, keepdims=True), (SLOTS, SLOTS))
    feature = jnp.transpose(feature)[:8, :]
    for peer in range(8):
        feat_ref[peer] = feature
    att_copy = pltpu.make_async_copy(att_ref, att_hbm, sem.at[0])
    att_copy.start()

    def backward(t, carry):
        rows = pl.ds(pl.multiple_of(t * TILE, TILE), TILE)
        key_t = jnp.transpose(kvs[rows, :HEAD_DIM])
        acc = jnp.zeros((TILE, HEAD_DIM), F32)
        for c in range(LANES // QCHUNK):
            lanes = slice(c * QCHUNK, (c + 1) * QCHUNK)
            slope = d_ref[rows, lanes].reshape(TILE // 8, 8, QCHUNK)
            w = w_ref[rows, lanes].astype(F32).reshape(TILE // 8, 8, QCHUNK)
            ds = (w * (slope - cen_ref[:, lanes][None]) * SCALE).reshape(TILE, QCHUNK).astype(BF)
            w_ref[rows, lanes] = ds
            acc += dot(ds, q_ref[lanes, :])
        dkv_ref[rows, :HEAD_DIM] = acc.astype(BF)
        dqt_ref[...] += dot(key_t, w_ref[rows, :])
        return carry

    lax.fori_loop(0, tiles, backward, 0)

    for h in range(HEADS):
        lanes = slice(h * HEAD_DIM, (h + 1) * HEAD_DIM)
        dq_ref[:, lanes] = jnp.transpose(dqt_ref[:, lanes].astype(BF))
    dq_copy = pltpu.make_async_copy(dq_ref, dq_hbm, sem.at[1])
    dq_copy.start()
    dkv_ref[pl.ds(pl.multiple_of(tiles * TILE, TILE), TILE), :] = jnp.zeros((TILE, 2 * HEAD_DIM), BF)
    for k, (far, near) in enumerate(((far0, near0), (far1, near1), (far2, near2), (far3, near3))):
        first = lax.rem(row + k, ROWS_Y) * ROWS_Z
        for out, steps in ((far, FAR), (near, NEAR)):
            for i, step in enumerate(steps):
                shard = first + lax.rem(col + step, ROWS_Z)
                rows = dkv_ref[pl.ds(pl.multiple_of(base_ref[shard], GROUP), SLOTS), :]
                out[i * SLOTS : (i + 1) * SLOTS, :] = jnp.where(shard <= own, rows, jnp.zeros_like(rows))
    att_copy.wait()
    dq_copy.wait()


def place_q_kernel(sel_ref, router_ref, att_ref, dq_ref, mixed_ref, qgrad_ref):
    place = one_hot(placer(sel_ref[...]))
    router = router_ref[...]
    for h in range(HEADS):
        lanes = slice(h * HEAD_DIM, (h + 1) * HEAD_DIM)
        mix = (router * att_ref[:, lanes].astype(F32)).astype(BF)
        mixed_ref[:, lanes] = dot(place, mix).astype(BF)
        qgrad_ref[:, lanes] = dot(place, dq_ref[:, lanes]).astype(BF)


def sum_of(*refs):
    total = refs[0][...].astype(F32)
    for ref in refs[1:]:
        total += ref[...].astype(F32)
    return total


def add_far_kernel(in0, in1, in2, in3, up_ref, down_ref, across_ref):
    total = sum_of(in0, in1, in2, in3).astype(BF)
    up_ref[...] = total[: 2 * SLOTS]
    down_ref[...] = total[2 * SLOTS : 4 * SLOTS]
    across_ref[...] = total[4 * SLOTS :]


def add_near_kernel(in0, in1, in2, in3, up_ref, down_ref, across_ref, own_ref, next_ref, prev_ref):
    total = sum_of(in0, in1, in2, in3)
    up = up_ref[...].astype(F32)
    down = down_ref[...].astype(F32)
    own_ref[...] = (total[:SLOTS] + up[:SLOTS] + down[:SLOTS] + across_ref[...].astype(F32)).astype(BF)
    next_ref[...] = (total[SLOTS : 2 * SLOTS] + up[SLOTS:]).astype(BF)
    prev_ref[...] = (total[2 * SLOTS :] + down[SLOTS:]).astype(BF)


def place_kv_kernel(sel_ref, router_ref, feat_ref, own_ref, prev_ref, next_ref, kgrad_ref, vgrad_ref, rgrad_ref):
    total = sum_of(own_ref, prev_ref, next_ref)
    placed = dot(one_hot(placer(sel_ref[...])), total.astype(BF)).astype(BF)
    kgrad_ref[...] = placed[:, :HEAD_DIM]
    vgrad_ref[...] = placed[:, HEAD_DIM:]
    feature = feat_ref[0]
    for k in range(1, 8):
        feature += feat_ref[k]
    router = router_ref[...]
    terms = router * (1.0 - router) * column_of(feature[:1, :])
    terms = jnp.concatenate([terms] * (TOK // SLOTS), axis=1)
    rgrad_ref[...] = jnp.sum(jnp.where(picker(sel_ref[...]), terms, 0.0), axis=0, keepdims=True)


def call(kernel, outs, args, scratch=(), specs=None, cost=None, limit=12 * 1024 * 1024, outside=0):
    return pl.pallas_call(
        kernel,
        out_shape=[jax.ShapeDtypeStruct(s, d) for s, d in outs],
        in_specs=specs or [pl.BlockSpec(memory_space=VMEM)] * len(args),
        out_specs=[pl.BlockSpec(memory_space=pltpu.HBM)] * outside + [pl.BlockSpec(memory_space=VMEM)] * (len(outs) - outside),
        scratch_shapes=list(scratch),
        compiler_params=pltpu.CompilerParams(vmem_limit_bytes=limit),
        cost_estimate=pl.CostEstimate(flops=cost[0], bytes_accessed=cost[1], transcendentals=0),
    )(*args)


def along_z(rows, step):
    return lax.ppermute(rows, "z", [(s, (s + step) % ROWS_Z) for s in range(ROWS_Z)])


def along_y(rows, step):
    return lax.ppermute(rows, "y", [(s, (s + step) % ROWS_Y) for s in range(ROWS_Y)])


def attend(pos, ow0, ow1, ow2, ow3, ev0, ev1, ev2, ev3, od0, od1, od2, od3, q, g, c):
    specs = [pl.BlockSpec(memory_space=pltpu.SMEM)] + [pl.BlockSpec(memory_space=VMEM)] * 15
    return call(
        attention_kernel,
        [((SLOTS, LANES), BF)] * 2 + [((len(FAR) * SLOTS, 2 * HEAD_DIM), BF)] * 4
        + [((len(NEAR) * SLOTS, 2 * HEAD_DIM), BF)] * 4 + [((8, 8, SLOTS), F32)],
        (pos, ow0, ow1, ow2, ow3, ev0, ev1, ev2, ev3, od0, od1, od2, od3, q, g, c),
        scratch=[
            VMEM((PACKED + TILE, 2 * HEAD_DIM), BF),
            VMEM((PACKED + TILE, 2 * HEAD_DIM), BF), VMEM((PACKED, LANES), F32), VMEM((PACKED, LANES), F32), VMEM((PACKED, LANES), BF),
            VMEM((HEAD_DIM, LANES), F32), VMEM((HEAD_DIM, LANES), F32),
            VMEM((8, LANES), F32), VMEM((8, LANES), F32), VMEM((8, LANES), F32),
            VMEM((PACKED // TILE, 8, LANES), F32),
            VMEM((SLOTS, LANES), BF), VMEM((SLOTS, LANES), BF),
            pltpu.SMEM((SHARDS,), jnp.int32),
            pltpu.SemaphoreType.DMA((2,)),
        ],
        specs=specs,
        cost=(12 * PACKED * LANES * HEAD_DIM, 8 << 20),
        limit=LIMIT, outside=2)


def shards(query_rows, key_rows, value_rows, cotangent, router_logits, selection):
    sel = selection.reshape(1, SLOTS)
    logits = router_logits.reshape(1, TOK)
    row = lax.axis_index("y")
    col = lax.axis_index("z")
    (own,) = call(select_kv_kernel, [((SLOTS, 2 * HEAD_DIM), BF)], (sel, key_rows, value_rows),
                  scratch=[VMEM((1, SLOTS), jnp.int32), VMEM((TOK, HEAD_DIM), BF), VMEM((TOK, HEAD_DIM), BF),
                           pltpu.SemaphoreType.DMA((3,))],
                  specs=[pl.BlockSpec(memory_space=pltpu.HBM)] * 3,
                  cost=(2 * SLOTS * TOK * 256, 1 << 20), limit=60 * 1024 * 1024)
    up = along_z(own, 2)
    down = along_z(own, 6)
    across = along_z(own, 4)
    owns = [own] + [along_y(own, k) for k in range(1, ROWS_Y)]
    near = along_z(jnp.concatenate([own, down], axis=0), 7)
    far = along_z(jnp.concatenate([up, own], axis=0), 1)
    even = jnp.concatenate([down, across, up], axis=0)
    evens = [even] + [along_y(even, k) for k in range(1, ROWS_Y)]
    odd = jnp.concatenate([near, far], axis=0)
    odds = [odd] + [along_y(odd, k) for k in range(1, ROWS_Y)]
    q, g, c, router = call(
        select_q_kernel,
        [((LANES, HEAD_DIM), BF)] * 3 + [((SLOTS, SLOTS), F32)],
        (sel, logits, query_rows, cotangent),
        cost=(4 * SLOTS * TOK * LANES, 3 << 20))
    pos = jnp.stack([row, col]).astype(jnp.int32)
    att, dq, *parts, feat = attend(pos, *owns, *evens, *odds, q, g, c)
    far = [parts[0]] + [along_y(parts[k], k) for k in range(1, ROWS_Y)]
    feat = lax.all_to_all(feat, "mp", 0, 0, tiled=True)
    mixed, qgrad = call(place_q_kernel, [((TOK, LANES), BF)] * 2, (sel, router, att, dq),
                        cost=(4 * SLOTS * TOK * LANES, 3 << 20))
    *waiting, feat = lax.optimization_barrier((*parts[5:], feat))
    near = [parts[4]] + [along_y(waiting[k - 1], k) for k in range(1, ROWS_Y)]
    pair, one = ((2 * SLOTS, 2 * HEAD_DIM), BF), ((SLOTS, 2 * HEAD_DIM), BF)
    up, down, across = call(add_far_kernel, [pair, pair, one], far, cost=(1 << 20, 2 << 20))
    across = along_z(across, 4)
    up = along_z(up, 2)
    down = along_z(down, 6)
    across, mixed, qgrad = lax.optimization_barrier((across, mixed, qgrad))
    own, nxt, prv = call(add_near_kernel, [one] * 3, (*near, up, down, across), cost=(1 << 20, 2 << 20))
    nxt, prv = along_z(nxt, 1), along_z(prv, 7)
    kgrad, vgrad, rgrad = call(
        place_kv_kernel,
        [((TOK, HEAD_DIM), BF)] * 2 + [((1, TOK), F32)],
        (sel, router, feat, own, nxt, prv),
        cost=(2 * SLOTS * TOK * 256, 1 << 20))
    return mixed, qgrad, kgrad, vgrad, rgrad.reshape(TOK)


def solution(mesh):
    inner = Mesh(mesh.devices.reshape(ROWS_Y, ROWS_Z, 8), ("y", "z", "mp"))
    seq = ("y", "z")
    in_specs = (P(seq, "mp"), P(seq, "mp"), P(seq, "mp"), P(seq, "mp"), P(seq), P(seq))
    out_specs = (P(seq, "mp"), P(seq, "mp"), P(seq, "mp"), P(seq, "mp"), P(seq))

    return jax.shard_map(shards, mesh=inner, in_specs=in_specs, out_specs=out_specs, check_vma=False)
```
